256 devices in a mesh: space: 64 (over z, x, core), freq: 4 (over y).
Axes of the slice: x: 4, y: 4, z: 8, core: 2. Of those that a mesh axis runs over, the one named last changes fastest.
Arguments:
- u_velocity: bfloat16 [2176, 128, 512], P(None, 'space', 'freq'), may hold values from -6 to 6
- v_velocity: bfloat16 [2176, 128, 512], P(None, 'space', 'freq'), may hold values from -6 to 6
- cell_weights: float32 [128, 512], P('space', 'freq'), may hold values from 0.25 to 4
- block_offsets: int32 [16], replicated, may hold values from 0 to 1920
- triads: int32 [64, 2], replicated, may hold values from 0 to 63
Outputs:
- eigen_values: float32 [64, 2], replicated
- mode_fields: float32 [64, 2, 128, 512], P(None, None, 'space', 'freq')
The draws below stay inside these ranges and needn't reach their ends.
Inputs may be any that keep to these rules, and one draw needn't show every extreme that they name: `triads`: k and l are each below 64, so k + l is below 128.
All inputs are finite; a program needn't handle non-finite values.
Results may differ from the reference program's by a relative error of at most 0.012.
Values may be sent and summed in bfloat16 or wider, within the bound.
A program may use at most 64 MiB of HBM per device.

```python
import math
import jax
import jax.numpy as jnp
from jax import lax

NFFT = 256
NB = 16
SX = 2
POW = 4
NT = 2176
NX = 128
NY = 512
NTRI = 64


def plant(drawn, rng, least, largest):
    dims = drawn.shape
    index_at = [jax.random.randint(jax.random.fold_in(rng, axis), (), 0, dims[axis]) for axis in range(len(dims))]
    drawn = drawn.at[tuple(index_at)].set(least)
    longest = dims.index(max(dims))
    index_at[longest] = (index_at[longest] + 1) % dims[longest]
    return drawn.at[tuple(index_at)].set(largest)


def block_scale(own_key, dims, shards, low, top_value):
    loudness = 1.0
    for position, parts in shards:
        steps = jax.random.uniform(jax.random.fold_in(jax.random.fold_in(own_key, 6), position), (parts,), jnp.float32, low / len(shards), top_value / len(shards))
        loudness = loudness * jnp.repeat(jnp.exp(steps), dims[position] // parts).reshape((-1,) + (1,) * (len(dims) - 1 - position))
    return loudness


def bell_draw(rng, dims, spread, limit, cuts=(), held_as=jnp.bfloat16):
    entries = jax.random.normal(rng, dims, jnp.float32) * spread
    if len(cuts) > 0:
        entries = block_scale(rng, dims, cuts, -0.22, 0.18) * entries
    return jnp.clip(entries, min=-limit, max=limit).astype(held_as)


def setup_inputs(seed: int = 0) -> dict:
    arg_keys = jax.random.split(jax.random.key(seed), 6)
    u_velocity = bell_draw(arg_keys[0], (NT, NX, NY), 1.0, 6.0, ((1, 64), (2, 4)))
    v_velocity = bell_draw(arg_keys[1], (NT, NX, NY), 1.0, 6.0, ((1, 64), (2, 4)))
    cell_weights = jnp.clip(jnp.exp(math.log(4.0) - 2.7725887 * jax.random.uniform(arg_keys[2], (NX, NY), jnp.float32) ** block_scale(arg_keys[2], (NX, NY), ((0, 64), (1, 4)), -0.2, 0.2)), 0.25, 4.0)
    block_offsets = plant(jax.random.randint(arg_keys[3], (NB,), 0, NT - NFFT + 1), jax.random.fold_in(arg_keys[3], 1), 0, NT - NFFT).astype(jnp.int32)
    triads = plant(jax.random.randint(arg_keys[4], (NTRI, 2), 0, NFFT // 4), jax.random.fold_in(arg_keys[4], 1), 0, (NFFT // 4) - 1).astype(jnp.int32)
    return {"u_velocity": u_velocity, "v_velocity": v_velocity, "cell_weights": cell_weights, "block_offsets": block_offsets, "triads": triads}


def make_table(length):
    half_len = length // 2
    times_idx = jnp.arange(length, dtype=jnp.int32)
    freq_idx = jnp.arange(half_len, dtype=jnp.int32)
    phases = freq_idx[:, None] * times_idx[None, :] % length
    angles = phases.astype(jnp.float32) * (2.0 * math.pi / length)
    window = 0.5 - 0.5 * jnp.cos(times_idx.astype(jnp.float32) * (2.0 * math.pi / length))
    scaling = 1.0 / jnp.sqrt(jnp.sum(window * window))
    transform = jnp.concatenate([jnp.cos(angles) * scaling, -jnp.sin(angles) * scaling], axis=0)
    return (window, transform.astype(jnp.bfloat16))

def spectra(vorticity, offsets):
    window, transform = make_table(NFFT)
    fluct = vorticity - lax.optimization_barrier(jnp.mean(vorticity, axis=0, keepdims=True))
    blocks = jax.vmap(lambda start: lax.dynamic_slice_in_dim(fluct, start, NFFT, 0))(offsets)
    windowed = (blocks * window[None, :, None, None]).astype(jnp.bfloat16)
    return jnp.einsum('ft,btxy->bfxy', transform.astype(jnp.float32), windowed.astype(jnp.float32), precision=lax.Precision.HIGHEST)

def pick_target(spectrum, triads):
    half_len = spectrum.shape[1] // 2
    target = triads[:, 0] + triads[:, 1]
    return (jnp.take(spectrum[:, :half_len], target, axis=1), jnp.take(spectrum[:, half_len:], target, axis=1))

def partial_sums(spectrum, weights, triads):
    half_len = spectrum.shape[1] // 2
    real_part = spectrum[:, :half_len]
    imag_part = spectrum[:, half_len:]
    first_re = jnp.take(real_part, triads[:, 0], axis=1)
    first_im = jnp.take(imag_part, triads[:, 0], axis=1)
    second_re = jnp.take(real_part, triads[:, 1], axis=1)
    second_im = jnp.take(imag_part, triads[:, 1], axis=1)
    target_re, target_im = pick_target(spectrum, triads)
    prod_re = (first_re * second_re - first_im * second_im) * weights
    prod_im = (first_re * second_im + first_im * second_re) * weights
    high = lax.Precision.HIGHEST
    cross_re = jnp.einsum('btxy,ctxy->tbc', prod_re, target_re, precision=high) + jnp.einsum('btxy,ctxy->tbc', prod_im, target_im, precision=high)
    cross_im = jnp.einsum('btxy,ctxy->tbc', prod_re, target_im, precision=high) - jnp.einsum('btxy,ctxy->tbc', prod_im, target_re, precision=high)
    return jnp.stack([cross_re, cross_im], axis=1)

def leading(matrices):
    high = lax.Precision.HIGHEST
    mat_re = matrices[:, 0]
    mat_im = matrices[:, 1]
    vec_re = jnp.full(mat_re.shape[:2], 1.0 / math.sqrt(mat_re.shape[1]), jnp.float32)
    vec_im = jnp.zeros(mat_re.shape[:2], jnp.float32)

    def apply(part_re, part_im):
        out_re = jnp.einsum('tbc,tc->tb', mat_re, part_re, precision=high) - jnp.einsum('tbc,tc->tb', mat_im, part_im, precision=high)
        out_im = jnp.einsum('tbc,tc->tb', mat_re, part_im, precision=high) + jnp.einsum('tbc,tc->tb', mat_im, part_re, precision=high)
        return (out_re, out_im)
    for repeat in range(POW):
        out_re, out_im = apply(vec_re, vec_im)
        length = jnp.sqrt(lax.optimization_barrier(jnp.sum(out_re * out_re + out_im * out_im, axis=1, keepdims=True)))
        vec_re = out_re / length
        vec_im = out_im / length
    out_re, out_im = apply(vec_re, vec_im)
    value_re = lax.optimization_barrier(jnp.sum(vec_re * out_re + vec_im * out_im, axis=1))
    value_im = lax.optimization_barrier(jnp.sum(vec_re * out_im - vec_im * out_re, axis=1))
    return (jnp.stack([vec_re, vec_im], axis=1), jnp.stack([value_re, value_im], axis=1))

def modes(vectors, target_re, target_im):
    high = lax.Precision.HIGHEST
    vec_re = vectors[:, 0]
    vec_im = vectors[:, 1]
    mode_re = jnp.einsum('tb,btxy->txy', vec_re, target_re, precision=high) - jnp.einsum('tb,btxy->txy', vec_im, target_im, precision=high)
    mode_im = jnp.einsum('tb,btxy->txy', vec_re, target_im, precision=high) + jnp.einsum('tb,btxy->txy', vec_im, target_re, precision=high)
    return jnp.stack([mode_re, mode_im], axis=1)

def reference(u_velocity, v_velocity, cell_weights, block_offsets, triads):
    u_padded = jnp.pad(u_velocity, ((0, 0), (0, 0), (1, 1)))
    v_padded = jnp.pad(v_velocity, ((0, 0), (1, 1), (0, 0)))

    def slab(index):
        start = (index * SX).astype(jnp.int32)
        u_part = lax.dynamic_slice_in_dim(u_padded, start, SX, 1).astype(jnp.float32)
        v_part = lax.dynamic_slice_in_dim(v_padded, start, SX + 2, 1).astype(jnp.float32)
        vorticity = 0.5 * (v_part[:, 2:, :] - v_part[:, :-2, :]) - 0.5 * (u_part[:, :, 2:] - u_part[:, :, :-2])
        weights = lax.dynamic_slice_in_dim(cell_weights, start, SX, 0)
        return (spectra(vorticity, block_offsets), weights)

    def accumulate(carry, index):
        spectrum, weights = slab(index)
        return (carry + partial_sums(spectrum, weights, triads), None)
    indices = jnp.arange(NX // SX, dtype=jnp.int32)
    total, _ = lax.scan(accumulate, jnp.zeros((NTRI, 2, NB, NB), jnp.float32), indices)
    total = total / (NB * math.sqrt(NX * NY))
    vectors, values = leading(total)

    def shape_mode(index):
        spectrum, weights = slab(index)
        target_re, target_im = pick_target(spectrum, triads)
        return modes(vectors, target_re, target_im)
    pieces = lax.map(shape_mode, indices)
    mode_fields = jnp.transpose(pieces, (1, 2, 0, 3, 4)).reshape(NTRI, 2, NX, NY)
    return (values, mode_fields)
```

```python
import math

import jax
import jax.numpy as jnp
import numpy as np
from jax import lax
from jax.experimental import pallas as pl
from jax.experimental.pallas import tpu as pltpu
from jax.sharding import PartitionSpec as P

NFFT = 256
HALF = NFFT // 2
NB = 16
POW = 4
NT = 2176
LANES = 128
NTRI = 64
NZ = 8
GROUP = 32
PER_Z = 8
NFREQ = 4
BATCH = 8
NBATCH = NTRI // BATCH
SUB = 64
CHUNKS = ((0, 512), (512, 512), (1024, 512), (1536, 640))
F32 = jnp.float32
BF16 = jnp.bfloat16


def tables():
    times = np.arange(NFFT)
    freqs = np.arange(HALF)
    angles = (freqs[:, None] * times[None, :] % NFFT).astype(np.float32) * np.float32(2.0 * math.pi / NFFT)
    window = (0.5 - 0.5 * np.cos(times * (2.0 * math.pi / NFFT))).astype(np.float32)
    scaling = np.float32(1.0 / np.sqrt(np.sum(window.astype(np.float64) ** 2)))
    transform = np.concatenate(
        [np.cos(angles.astype(np.float64)) * scaling, -np.sin(angles.astype(np.float64)) * scaling], axis=0
    )
    hann = np.ascontiguousarray(np.broadcast_to(window[:, None], (NFFT, LANES)))
    small = np.zeros((160, LANES), np.float32)
    for lane in range(LANES):
        if lane + 1 < LANES:
            small[lane + 1, lane] += 0.5
        if lane > 0:
            small[lane - 1, lane] -= 0.5
    small[128, 0] = 1.0
    small[129, LANES - 1] = 1.0
    small[144 + 1, 0] = -0.5
    small[144 + 8, LANES - 1] = 0.5
    return transform.astype(jnp.bfloat16), hann, small.astype(jnp.bfloat16)


def dot_nt(lhs, rhs):
    return lax.dot_general(lhs, rhs, (((1,), (1,)), ((), ())), preferred_element_type=F32)


def dot_nn(lhs, rhs):
    return lax.dot_general(lhs, rhs, (((1,), (0,)), ((), ())), preferred_element_type=F32)


def split(value):
    high = value.astype(BF16)
    return high, (value - high.astype(F32)).astype(BF16)


def swap16(value, lane):
    return jnp.where(
        (lane // 16) % 2 == 0, pltpu.roll(value, LANES - 16, value.ndim - 1), pltpu.roll(value, 16, value.ndim - 1)
    )


def kernel(
    u_hbm, v_hbm, table_hbm, hann_hbm, small_hbm, w_ref, offs, tri,
    modes_ref, vals_ref,
    ubuf, vbuf, table, hann, small, vf, duf, snd, halo, colsend, colrecv, vort, spec,
    lhi, llo, rhi, rlo, cross, pieces, recv1, recv2, recv3, out3,
    load_sem, vsend, vrecv, usend, urecv, s1, r1, s2, r2, s3, r3,
):
    sp = lax.axis_index("space")
    fq = lax.axis_index("freq")
    core = sp % 2
    zi = sp // PER_Z
    inz = sp % PER_Z
    me = inz * NFREQ + fq
    sibling = sp + 1 - 2 * core
    outer = (sp + 63 + 2 * core) % 64
    left = (fq + NFREQ - 1) % NFREQ
    right = (fq + 1) % NFREQ
    x_slow = core
    x_fast = 1 - core
    sign = (1 - 2 * core).astype(F32)

    loads_v = []
    for n, (t0, cnt) in enumerate(CHUNKS):
        rows = pl.ds(2 * t0, 2 * cnt)
        loads_v.append(pltpu.make_async_copy(v_hbm.at[rows], vbuf.at[rows], load_sem.at[n]))
        loads_v[-1].start()
    load_u = pltpu.make_async_copy(u_hbm, ubuf, load_sem.at[4])
    load_s = pltpu.make_async_copy(small_hbm, small, load_sem.at[5])
    load_h = pltpu.make_async_copy(hann_hbm, hann, load_sem.at[6])
    load_t = pltpu.make_async_copy(table_hbm, table, load_sem.at[7])
    load_u.start()
    load_s.start()
    load_h.start()
    load_t.start()

    barrier = pltpu.get_barrier_semaphore()
    pl.semaphore_signal(barrier, inc=1, device_id={"space": outer, "freq": fq}, device_id_type=pl.DeviceIdType.MESH)

    @pl.loop(1, GROUP)
    def _(d):
        q = (me + d) % GROUP
        pl.semaphore_signal(
            barrier, inc=1, device_id={"space": zi * PER_Z + q // NFREQ, "freq": q % NFREQ},
            device_id_type=pl.DeviceIdType.MESH,
        )

    @pl.loop(1, NZ)
    def _(d):
        z = (zi + d) % NZ
        pl.semaphore_signal(
            barrier, inc=1, device_id={"space": z * PER_Z + inz, "freq": fq}, device_id_type=pl.DeviceIdType.MESH
        )

    copies_v = []
    for n, (t0, cnt) in enumerate(CHUNKS):
        loads_v[n].wait()

        @pl.loop(t0 // SUB, (t0 + cnt) // SUB)
        def _(i):
            both = pl.ds(pl.multiple_of(i * 2 * SUB, 2 * SUB), 2 * SUB)
            one = pl.ds(pl.multiple_of(i * SUB, SUB), SUB)
            vf[both, :] = vbuf[both, :].astype(F32)
            snd[1, one, :] = vf[pl.ds(i * 2 * SUB + x_slow, SUB, stride=2), :].astype(BF16)
            snd[0, one, :] = vf[pl.ds(i * 2 * SUB + x_fast, SUB, stride=2), :].astype(BF16)

        if n == 0:
            pl.semaphore_wait(barrier, GROUP - 1 + NZ - 1 + 1)
        for plane, target in ((1, outer), (0, sibling)):
            rows = pl.ds(t0, cnt)
            copies_v.append(
                pltpu.make_async_remote_copy(
                    src_ref=snd.at[plane, rows], dst_ref=halo.at[plane, rows],
                    send_sem=vsend.at[plane, n], recv_sem=vrecv.at[plane, n],
                    device_id={"space": target, "freq": fq}, device_id_type=pl.DeviceIdType.MESH,
                )
            )
            copies_v[-1].start()

    load_u.wait()
    load_s.wait()
    pick = small[128:144, :]

    @pl.loop(0, 2 * NT // 256)
    def _(i):
        rows = pl.ds(pl.multiple_of(i * 256, 256), 256)
        colsend[:, rows] = dot_nt(pick, ubuf[rows, :])[:8]

    copies_u = []
    for slot, target in ((1, left), (0, right)):
        copies_u.append(
            pltpu.make_async_remote_copy(
                src_ref=colsend, dst_ref=colrecv.at[slot], send_sem=usend.at[slot], recv_sem=urecv.at[slot],
                device_id={"space": sp, "freq": target}, device_id_type=pl.DeviceIdType.MESH,
            )
        )
        copies_u[-1].start()
    for copy in copies_u:
        copy.wait()
    row = lax.broadcasted_iota(jnp.int32, (16, LANES), 0)
    keep = jnp.where(row < 8, (fq > 0).astype(F32), (fq < NFREQ - 1).astype(F32))
    edge = (small[144:160, :].astype(F32) * keep).astype(BF16)
    diff = small[0:128, :]

    @pl.loop(0, 2 * NT // 256)
    def _(i):
        rows = pl.ds(pl.multiple_of(i * 256, 256), 256)
        cols = jnp.concatenate([colrecv[0, :, rows], colrecv[1, :, rows]], axis=0)
        duf[rows, :] = dot_nn(ubuf[rows, :], diff) + dot_nn(cols.T.astype(BF16), edge)

    load_h.wait()
    load_t.wait()
    lane = lax.broadcasted_iota(jnp.int32, (16, LANES), 1)
    quarter = lane // 32
    has_outer = jnp.where(core == 0, sp > 0, sp < 63).astype(F32)

    spectra_by_f = spec.reshape(2, NFFT, NB, LANES)
    for plane in (0, 1):
        own = x_fast if plane == 0 else x_slow
        other = x_slow if plane == 0 else x_fast
        half = 0.5 * sign if plane == 0 else -0.5 * sign
        mask = 1.0 if plane == 0 else has_outer
        total = jnp.zeros((8, LANES), F32)
        for n, (t0, cnt) in enumerate(CHUNKS):
            copies_v[2 * n + 1 - plane].wait()

            def vorticity(i, total):
                one = pl.ds(pl.multiple_of(i * SUB, SUB), SUB)
                far = halo[plane, one, :].astype(F32) * mask
                near = vf[pl.ds(i * 2 * SUB + other, SUB, stride=2), :]
                value = half * (far - near) - duf[pl.ds(i * 2 * SUB + own, SUB, stride=2), :]
                vort[plane, one, :] = value
                return total + jnp.sum(value.reshape(SUB // 8, 8, LANES), axis=0)

            total = lax.fori_loop(t0 // SUB, (t0 + cnt) // SUB, vorticity, total)
        mean = jnp.sum(total, axis=0, keepdims=True) * (1.0 / NT)

        @pl.loop(0, NB // 2)
        def _(pair):
            parts = []
            for k in (0, 1):
                block = vort[plane, pl.ds(offs[2 * pair + k], NFFT), :]
                parts.append(((block - mean) * hann[...]).astype(BF16))
            out = dot_nn(table[...], jnp.concatenate(parts, axis=1))
            for k in (0, 1):
                spec[plane, pl.ds(2 * pair + k, NFFT, stride=NB), :] = out[:, k * LANES:(k + 1) * LANES]

        weight = w_ref[pl.ds(own, 1), :]

        @pl.loop(0, NBATCH)
        def _(batch):
            for i in range(BATCH):
                j = batch * BATCH + i
                k_at = tri[0, j]
                l_at = tri[1, j]

                def rows_of(f):
                    return spectra_by_f[plane, f]

                k_re, k_im = rows_of(k_at), rows_of(k_at + HALF)
                l_re, l_im = rows_of(l_at), rows_of(l_at + HALF)
                t_re, t_im = rows_of(k_at + l_at), rows_of(k_at + l_at + HALF)
                p_re = (k_re * l_re - k_im * l_im) * weight
                p_im = (k_re * l_im + k_im * l_re) * weight
                at = slice(i * NB, (i + 1) * NB)
                for c, value in ((0, p_re), (1, p_im)):
                    high, low = split(value)
                    lhi[at, c * LANES:(c + 1) * LANES] = high
                    llo[at, c * LANES:(c + 1) * LANES] = low
                re_hi, re_lo = split(t_re)
                im_hi, im_lo = split(t_im)
                at_re = slice(2 * i * NB, (2 * i + 1) * NB)
                at_im = slice((2 * i + 1) * NB, (2 * i + 2) * NB)
                rhi[plane, batch, at_re, 0:LANES] = re_hi
                rhi[plane, batch, at_im, 0:LANES] = im_hi
                rhi[plane, batch, at_re, LANES:] = im_hi
                rhi[plane, batch, at_im, LANES:] = -re_hi
                rlo[at_re, 0:LANES] = re_lo
                rlo[at_im, 0:LANES] = im_lo
                rlo[at_re, LANES:] = im_lo
                rlo[at_im, LANES:] = -re_lo
            right_hi = rhi[plane, batch]
            out = dot_nt(lhi[...], right_hi) + dot_nt(llo[...], right_hi) + dot_nt(lhi[...], rlo[...])
            for h in (0, 1):
                cols = slice(h * LANES, (h + 1) * LANES)
                acc = out[h * 64:h * 64 + 16, cols]
                for i in (1, 2, 3):
                    acc = jnp.where(quarter == i, out[h * 64 + i * 16:h * 64 + i * 16 + 16, cols], acc)
                if plane == 0:
                    cross[2 * batch + h] = acc
                else:
                    acc = acc + cross[2 * batch + h]
                    low, high = acc[0:8], acc[8:16]
                    first = lane[0:8] < 64
                    pieces[4 * batch + 2 * h] = jnp.where(first, low, pltpu.roll(high, 64, 1))
                    pieces[4 * batch + 2 * h + 1] = jnp.where(first, pltpu.roll(low, 64, 1), high)

    @pl.loop(1, GROUP)
    def _(d):
        q = (me + d) % GROUP
        pltpu.make_async_remote_copy(
            src_ref=pieces.at[q], dst_ref=recv1.at[d - 1], send_sem=s1, recv_sem=r1,
            device_id={"space": zi * PER_Z + q // NFREQ, "freq": q % NFREQ}, device_id_type=pl.DeviceIdType.MESH,
        ).start()

    pltpu.make_async_copy(recv1, recv1, r1).wait()
    own_sum = pieces[me]
    for d in range(GROUP - 1):
        own_sum = own_sum + recv1[d]
    recv2[zi] = own_sum

    @pl.loop(1, NZ)
    def _(d):
        z = (zi + d) % NZ
        pltpu.make_async_remote_copy(
            src_ref=recv2.at[zi], dst_ref=recv2.at[zi], send_sem=s2, recv_sem=r2,
            device_id={"space": z * PER_Z + inz, "freq": fq}, device_id_type=pl.DeviceIdType.MESH,
        ).start()

    pltpu.make_async_copy(recv2.at[pl.ds(0, NZ - 1)], recv2.at[pl.ds(0, NZ - 1)], r2).wait()
    both = recv2[0]
    for z in range(1, NZ):
        both = both + recv2[z]
    both = both * (1.0 / (NB * math.sqrt(128 * 512)))

    c16 = jnp.concatenate([both, pltpu.roll(both, 64, 1)], axis=0)
    c16 = jnp.where(lane < 64, c16, 0.0)
    odd = (lane // 16) % 2 == 1
    mat = jnp.concatenate([jnp.where(odd, -c16, c16), swap16(c16, lane)], axis=0)
    turned = jnp.concatenate([mat, jnp.zeros((96, LANES), F32)], axis=0).T
    lane32 = lax.broadcasted_iota(jnp.int32, (32, LANES), 1)
    row32 = lax.broadcasted_iota(jnp.int32, (32, LANES), 0)
    lane1 = lax.broadcasted_iota(jnp.int32, (1, LANES), 1)
    mat_t = jnp.where(lane32 < 32, turned[0:32], pltpu.roll(turned[32:64], 32, 1))

    def by_triad(value, lanes):
        first = jnp.sum(jnp.where(lanes < 32, value, 0.0), axis=1, keepdims=True)
        second = jnp.sum(jnp.where((lanes >= 32) & (lanes < 64), value, 0.0), axis=1, keepdims=True)
        return jnp.where(lanes < 32, first, second)

    def to_lanes(vec):
        return jnp.sum(mat_t * vec, axis=0, keepdims=True)

    vec = jnp.where(row32 < 16, 1.0 / math.sqrt(NB), 0.0).astype(F32)
    for _ in range(POW // 2):
        out = to_lanes(vec)
        out = out / jnp.sqrt(by_triad(out * out, lane1))
        vec = by_triad(mat * out, lane32)
        vec = vec / jnp.sqrt(jnp.sum(vec * vec, axis=0, keepdims=True))
    out = to_lanes(vec)
    lead = jnp.where(lane1 < 64, jnp.sum(jnp.where(lane32 % 32 == row32, vec, 0.0), axis=0, keepdims=True), 0.0)
    val_re = by_triad(lead * out, lane1)
    crossed = lead * swap16(out, lane1)
    val_im = by_triad(jnp.where((lane1 // 16) % 2 == 0, crossed, -crossed), lane1)
    spot = lane1 - 2 * me
    re0, re1 = val_re[:, 0:1], val_re[:, 32:33]
    im0, im1 = val_im[:, 0:1], val_im[:, 32:33]
    vals = jnp.where(spot == 0, re0, jnp.where(spot == 1, re1, 0.0))
    vals = vals + jnp.where(spot == 64, im0, jnp.where(spot == 65, im1, 0.0))
    placed = jnp.where((me % 2) == 1, pltpu.roll(lead, 64, 1), lead)
    out3[...] = jnp.concatenate([placed, vals], axis=0)
    recv3[me] = out3[...]

    @pl.loop(1, GROUP)
    def _(d):
        q = (me + d) % GROUP
        pltpu.make_async_remote_copy(
            src_ref=out3, dst_ref=recv3.at[me], send_sem=s3, recv_sem=r3,
            device_id={"space": zi * PER_Z + q // NFREQ, "freq": q % NFREQ}, device_id_type=pl.DeviceIdType.MESH,
        ).start()

    pltpu.make_async_copy(recv3.at[pl.ds(0, GROUP - 1)], recv3.at[pl.ds(0, GROUP - 1)], r3).wait()
    vals_all = recv3[0][1:2]
    for q in range(1, GROUP):
        vals_all = vals_all + recv3[q][1:2]
    vals_ref[...] = vals_all

    row_lhs = lax.broadcasted_iota(jnp.int32, (16, 2 * LANES), 0)
    lane_lhs = lax.broadcasted_iota(jnp.int32, (16, 2 * LANES), 1)
    live = lane_lhs // 32 == row_lhs // 2

    @pl.loop(0, NBATCH)
    def _(batch):
        parts = [recv3[4 * batch + 2 * h][0:1] + recv3[4 * batch + 2 * h + 1][0:1] for h in (0, 1)]
        flat = jnp.concatenate([jnp.where((lane1 // 16) % 2 == 1, -p, p) for p in parts], axis=1)
        turned = jnp.concatenate([swap16(p, lane1) for p in parts], axis=1)
        coeff = jnp.where(live, jnp.where(row_lhs % 2 == 0, flat, turned), 0.0)
        high, low = split(coeff)
        stacked = jnp.concatenate([high, low], axis=0)
        fields = jnp.concatenate([rhi[0, batch, :, 0:LANES], rhi[1, batch, :, 0:LANES]], axis=1)
        res = dot_nn(stacked, fields)
        res = res[0:16] + res[16:32]
        modes_ref[pl.ds(batch * 32 + x_fast, 16, stride=2), :] = res[:, 0:LANES]
        modes_ref[pl.ds(batch * 32 + x_slow, 16, stride=2), :] = res[:, LANES:]

    pltpu.make_async_copy(recv1, recv1, s1).wait()
    pltpu.make_async_copy(recv2.at[pl.ds(0, NZ - 1)], recv2.at[pl.ds(0, NZ - 1)], s2).wait()
    pltpu.make_async_copy(recv3.at[pl.ds(0, GROUP - 1)], recv3.at[pl.ds(0, GROUP - 1)], s3).wait()


def on_device(u_velocity, v_velocity, cell_weights, block_offsets, triads):
    transform, hann, small = tables()
    u_rows = u_velocity.reshape(2 * NT, LANES)
    v_rows = v_velocity.reshape(2 * NT, LANES)
    anywhere = pl.BlockSpec(memory_space=pltpu.HBM)
    vmem = pl.BlockSpec(memory_space=pltpu.VMEM)
    smem = pl.BlockSpec(memory_space=pltpu.SMEM)
    dma = pltpu.SemaphoreType.DMA
    fields, values = pl.pallas_call(
        kernel,
        out_shape=(jax.ShapeDtypeStruct((4 * NTRI, LANES), F32), jax.ShapeDtypeStruct((1, LANES), F32)),
        in_specs=[anywhere] * 5 + [vmem, smem, smem],
        out_specs=(vmem, vmem),
        scratch_shapes=[
            pltpu.VMEM((2 * NT, LANES), BF16),
            pltpu.VMEM((2 * NT, LANES), BF16),
            pltpu.VMEM((NFFT, NFFT), BF16),
            pltpu.VMEM((NFFT, LANES), F32),
            pltpu.VMEM((160, LANES), BF16),
            pltpu.VMEM((2 * NT, LANES), F32),
            pltpu.VMEM((2 * NT, LANES), F32),
            pltpu.VMEM((2, NT, LANES), BF16),
            pltpu.VMEM((2, NT, LANES), BF16),
            pltpu.VMEM((8, 2 * NT), F32),
            pltpu.VMEM((2, 8, 2 * NT), F32),
            pltpu.VMEM((2, NT, LANES), F32),
            pltpu.VMEM((2, NFFT * NB, LANES), F32),
            pltpu.VMEM((BATCH * NB, 2 * LANES), BF16),
            pltpu.VMEM((BATCH * NB, 2 * LANES), BF16),
            pltpu.VMEM((2, NBATCH, 2 * BATCH * NB, 2 * LANES), BF16),
            pltpu.VMEM((2 * BATCH * NB, 2 * LANES), BF16),
            pltpu.VMEM((2 * NBATCH, NB, LANES), F32),
            pltpu.VMEM((GROUP, 8, LANES), F32),
            pltpu.VMEM((GROUP - 1, 8, LANES), F32),
            pltpu.VMEM((NZ, 8, LANES), F32),
            pltpu.VMEM((GROUP, 2, LANES), F32),
            pltpu.VMEM((2, LANES), F32),
            dma((8,)),
            dma((2, 4)), dma((2, 4)), dma((2,)), dma((2,)),
            dma(()), dma(()), dma(()), dma(()), dma(()), dma(()),
        ],
        compiler_params=pltpu.CompilerParams(
            collective_id=0, has_side_effects=True, vmem_limit_bytes=48 * 1024 * 1024
        ),
        name="bispectrum",
    )(u_rows, v_rows, transform, hann, small, cell_weights, block_offsets, triads.T)
    return values.reshape(2, NTRI).T, fields.reshape(NTRI, 2, 2, LANES)


def solution(mesh):
    return jax.shard_map(
        on_device,
        mesh=mesh,
        in_specs=(P(None, "space", "freq"), P(None, "space", "freq"), P("space", "freq"), P(), P()),
        out_specs=(P(), P(None, None, "space", "freq")),
        check_vma=False,
    )
```

```python
import math

import jax
import jax.numpy as jnp
import numpy as np
from jax import lax
from jax.experimental import pallas as pl
from jax.experimental.pallas import tpu as pltpu
from jax.sharding import PartitionSpec as P

NFFT = 256
HALF = NFFT // 2
NB = 16
POW = 4
NT = 2176
LANES = 128
NTRI = 64
NZ = 8
GROUP = 32
PER_Z = 8
NFREQ = 4
BATCH = 8
NBATCH = NTRI // BATCH
SUB = 64
CHUNKS = ((0, 512), (512, 512), (1024, 512), (1536, 640))
F32 = jnp.float32
BF16 = jnp.bfloat16


def tables():
    times = np.arange(NFFT)
    freqs = np.arange(HALF)
    angles = (freqs[:, None] * times[None, :] % NFFT).astype(np.float32) * np.float32(2.0 * math.pi / NFFT)
    window = (0.5 - 0.5 * np.cos(times * (2.0 * math.pi / NFFT))).astype(np.float32)
    scaling = np.float32(1.0 / np.sqrt(np.sum(window.astype(np.float64) ** 2)))
    transform = np.concatenate(
        [np.cos(angles.astype(np.float64)) * scaling, -np.sin(angles.astype(np.float64)) * scaling], axis=0
    )
    hann = np.ascontiguousarray(np.broadcast_to(window[:, None], (NFFT, LANES)))
    small = np.zeros((160, LANES), np.float32)
    for lane in range(LANES):
        if lane + 1 < LANES:
            small[lane + 1, lane] += 0.5
        if lane > 0:
            small[lane - 1, lane] -= 0.5
    small[128, 0] = 1.0
    small[129, LANES - 1] = 1.0
    small[144, 0] = -0.5
    small[145, LANES - 1] = 0.5
    return transform.astype(jnp.bfloat16), hann, small.astype(jnp.bfloat16)


def dot_nt(lhs, rhs):
    return lax.dot_general(lhs, rhs, (((1,), (1,)), ((), ())), preferred_element_type=F32)


def dot_nn(lhs, rhs):
    return lax.dot_general(lhs, rhs, (((1,), (0,)), ((), ())), preferred_element_type=F32)


def split(value):
    high = value.astype(BF16)
    return high, (value - high.astype(F32)).astype(BF16)


def swap16(value, lane):
    return jnp.where(
        (lane // 16) % 2 == 0, pltpu.roll(value, LANES - 16, value.ndim - 1), pltpu.roll(value, 16, value.ndim - 1)
    )


def kernel(
    u_hbm, v_hbm, table_hbm, hann_hbm, small_hbm, w_ref, offs, tri,
    modes_ref, vals_ref,
    ubuf, vbuf, table, hann, small, vf, duf, snd, halo, colsend, colrecv, vort, spec,
    lhs, rhi, rlo, cross, pieces, recv1, recv2, recv3, out3,
    load_sem, vsend, vrecv, usend, urecv, s1, r1, s2, r2, s3, r3,
):
    sp = lax.axis_index("space")
    fq = lax.axis_index("freq")
    core = sp % 2
    zi = sp // PER_Z
    xi = (sp // 2) % 4
    inz = sp % PER_Z
    me = inz * NFREQ + fq
    sibling = sp + 1 - 2 * core
    outer = (sp + 63 + 2 * core) % 64
    cores = [core, 1 - core]
    xs = [xi] + [(xi + d) % 4 for d in (1, 2, 3)]
    ys = [fq] + [(fq + d) % NFREQ for d in (1, 2, 3)]
    zs = [zi] + [(zi + d) % NZ for d in range(1, NZ)]
    x_slow = core
    x_fast = 1 - core
    sign = (1 - 2 * core).astype(F32)

    def device(space, freq):
        return {"device_id": {"space": space, "freq": freq}, "device_id_type": pl.DeviceIdType.MESH}

    loads_v = []
    for n, (t0, cnt) in enumerate(CHUNKS):
        rows = pl.ds(2 * t0, 2 * cnt)
        loads_v.append(pltpu.make_async_copy(v_hbm.at[rows], vbuf.at[rows], load_sem.at[n]))
    load_u = pltpu.make_async_copy(u_hbm, ubuf, load_sem.at[4])
    load_s = pltpu.make_async_copy(small_hbm, small, load_sem.at[5])
    load_h = pltpu.make_async_copy(hann_hbm, hann, load_sem.at[6])
    load_t = pltpu.make_async_copy(table_hbm, table, load_sem.at[7])
    load_s.start()
    loads_v[0].start()
    load_u.start()
    for load in loads_v[1:]:
        load.start()
    load_h.start()
    load_t.start()

    barrier = pltpu.get_barrier_semaphore()
    pl.semaphore_signal(barrier, inc=1, **device(outer, fq))
    for dz in (4, 3, 5, 2, 6, 1, 7):
        pl.semaphore_signal(barrier, inc=1, **device(zs[dz] * PER_Z + inz, fq))
    plane_spaces = {(dx, dc): zi * PER_Z + xs[dx] * 2 + cores[dc] for dx in range(4) for dc in (0, 1)}
    far_first = sorted(
        ((dx, dc, dy) for dx in range(4) for dc in (0, 1) for dy in range(4) if dx or dc or dy),
        key=lambda step: -(min(step[0], 4 - step[0]) + min(step[2], 4 - step[2])),
    )
    for dx, dc, dy in far_first:
        pl.semaphore_signal(barrier, inc=1, **device(plane_spaces[dx, dc], ys[dy]))

    def unpack(n):
        t0, cnt = CHUNKS[n]
        loads_v[n].wait()

        @pl.loop(t0 // SUB, (t0 + cnt) // SUB)
        def _(i):
            both = pl.ds(pl.multiple_of(i * 2 * SUB, 2 * SUB), 2 * SUB)
            one = pl.ds(pl.multiple_of(i * SUB, SUB), SUB)
            vf[both, :] = vbuf[both, :].astype(F32)
            snd[1, one, :] = vf[pl.ds(i * 2 * SUB + x_slow, SUB, stride=2), :].astype(BF16)
            snd[0, one, :] = vf[pl.ds(i * 2 * SUB + x_fast, SUB, stride=2), :].astype(BF16)

    copies_v = {}

    def send(n, plane, target):
        rows = pl.ds(CHUNKS[n][0], CHUNKS[n][1])
        copies_v[n, plane] = pltpu.make_async_remote_copy(
            src_ref=snd.at[plane, rows], dst_ref=halo.at[plane, rows],
            send_sem=vsend.at[plane, n], recv_sem=vrecv.at[plane, n], **device(target, fq),
        )
        copies_v[n, plane].start()

    load_s.wait()
    pick = small[128:144, :]
    unpack(0)
    load_u.wait()

    @pl.loop(0, 2 * NT // 256)
    def _(i):
        rows = pl.ds(pl.multiple_of(i * 256, 256), 256)
        cols = dot_nt(pick, ubuf[rows, :])
        colsend[0, :, rows] = cols[0:1]
        colsend[1, :, rows] = cols[1:2]

    pl.semaphore_wait(barrier, GROUP - 1 + NZ - 1 + 1)
    copies_u = []
    for slot, target in ((1, ys[3]), (0, ys[1])):
        copies_u.append(
            pltpu.make_async_remote_copy(
                src_ref=colsend.at[1 - slot], dst_ref=colrecv.at[slot],
                send_sem=usend.at[slot], recv_sem=urecv.at[slot], **device(sp, target),
            )
        )
        copies_u[-1].start()
    for n in range(len(CHUNKS)):
        if n > 0:
            unpack(n)
        send(n, 1, outer)
        send(n, 0, sibling)

    row = lax.broadcasted_iota(jnp.int32, (16, LANES), 0)
    keep = jnp.where(row == 0, (fq > 0).astype(F32), (fq < NFREQ - 1).astype(F32))
    edge = (small[144:160, :].astype(F32) * keep).astype(BF16)
    diff = small[0:128, :]
    row8 = lax.broadcasted_iota(jnp.int32, (16, 256), 0)
    for copy in copies_u:
        copy.wait()

    @pl.loop(0, 2 * NT // 256)
    def _(i):
        rows = pl.ds(pl.multiple_of(i * 256, 256), 256)
        cols = jnp.where(row8 == 0, colrecv[0, :, rows], jnp.where(row8 == 1, colrecv[1, :, rows], 0.0))
        duf[rows, :] = dot_nn(ubuf[rows, :], diff) + dot_nn(cols.T.astype(BF16), edge)

    load_h.wait()
    load_t.wait()
    lane = lax.broadcasted_iota(jnp.int32, (16, LANES), 1)
    quarter = lane // 32
    has_outer = jnp.where(core == 0, sp > 0, sp < 63).astype(F32)

    spectra_by_f = spec.reshape(2, NFFT, NB, LANES)
    for plane in (0, 1):
        own = x_fast if plane == 0 else x_slow
        other = x_slow if plane == 0 else x_fast
        half = 0.5 * sign if plane == 0 else -0.5 * sign
        mask = 1.0 if plane == 0 else has_outer
        total = jnp.zeros((8, LANES), F32)
        for n, (t0, cnt) in enumerate(CHUNKS):
            copies_v[n, plane].wait()

            def vorticity(i, total):
                one = pl.ds(pl.multiple_of(i * SUB, SUB), SUB)
                far = halo[plane, one, :].astype(F32) * mask
                near = vf[pl.ds(i * 2 * SUB + other, SUB, stride=2), :]
                value = half * (far - near) - duf[pl.ds(i * 2 * SUB + own, SUB, stride=2), :]
                vort[plane, one, :] = value
                return total + jnp.sum(value.reshape(SUB // 8, 8, LANES), axis=0)

            total = lax.fori_loop(t0 // SUB, (t0 + cnt) // SUB, vorticity, total)
        mean = jnp.sum(total, axis=0, keepdims=True) * (1.0 / NT)

        @pl.loop(0, NB // 4)
        def _(four):
            for h in (0, 1):
                parts = []
                for k in (0, 1):
                    block = vort[plane, pl.ds(offs[4 * four + 2 * h + k], NFFT), :]
                    parts.append(((block - mean) * hann[...]).astype(BF16))
                out = dot_nn(table[...], jnp.concatenate(parts, axis=1))
                for k in (0, 1):
                    spec[plane, pl.ds(4 * four + 2 * h + k, NFFT, stride=NB), :] = out[:, k * LANES:(k + 1) * LANES]

        weight = w_ref[pl.ds(own, 1), :]

        @pl.loop(0, 4)
        def _(step):
            x_to = (xi + 3 - step) % 4
            for dc in (1, 0):
                batch = x_to * 2 + cores[dc]
                for i in range(BATCH):
                    j = batch * BATCH + i
                    k_at = tri[0, j]
                    l_at = tri[1, j]
                    k_re, k_im = spectra_by_f[plane, k_at], spectra_by_f[plane, k_at + HALF]
                    l_re, l_im = spectra_by_f[plane, l_at], spectra_by_f[plane, l_at + HALF]
                    t_re, t_im = spectra_by_f[plane, k_at + l_at], spectra_by_f[plane, k_at + l_at + HALF]
                    p_re = (k_re * l_re - k_im * l_im) * weight
                    p_im = (k_re * l_im + k_im * l_re) * weight
                    for c, value in ((0, p_re), (1, p_im)):
                        high, low = split(value)
                        lhs[dc, i * NB:(i + 1) * NB, c * LANES:(c + 1) * LANES] = high
                        lhs[dc, 128 + i * NB:128 + (i + 1) * NB, c * LANES:(c + 1) * LANES] = low
                    re_hi, re_lo = split(t_re)
                    im_hi, im_lo = split(t_im)
                    at_re = slice(2 * i * NB, (2 * i + 1) * NB)
                    at_im = slice((2 * i + 1) * NB, (2 * i + 2) * NB)
                    rhi[plane, batch, at_re, 0:LANES] = re_hi
                    rhi[plane, batch, at_im, 0:LANES] = im_hi
                    rhi[plane, batch, at_re, LANES:] = im_hi
                    rhi[plane, batch, at_im, LANES:] = -re_hi
                    rlo[dc, at_re, 0:LANES] = re_lo
                    rlo[dc, at_im, 0:LANES] = im_lo
                    rlo[dc, at_re, LANES:] = im_lo
                    rlo[dc, at_im, LANES:] = -re_lo
                out = dot_nt(lhs[dc], rhi[plane, batch])
                out = out[0:128] + out[128:256] + dot_nt(lhs[dc, 0:128], rlo[dc])
                for h in (0, 1):
                    cols = slice(h * LANES, (h + 1) * LANES)
                    acc = out[h * 64:h * 64 + 16, cols]
                    for i in (1, 2, 3):
                        acc = jnp.where(quarter == i, out[h * 64 + i * 16:h * 64 + i * 16 + 16, cols], acc)
                    if plane == 0:
                        cross[2 * batch + h] = acc
                    else:
                        acc = acc + cross[2 * batch + h]
                        low, high = acc[0:8], acc[8:16]
                        first = lane[0:8] < 64
                        pieces[4 * batch + 2 * h] = jnp.where(first, low, pltpu.roll(high, 64, 1))
                        pieces[4 * batch + 2 * h + 1] = jnp.where(first, pltpu.roll(low, 64, 1), high)
                if plane == 1:
                    for dy in (2, 1, 3, 0):
                        copy = pltpu.make_async_remote_copy(
                            src_ref=pieces.at[4 * batch + ys[dy]], dst_ref=recv1.at[(3 - step) * 8 + dc * 4 + dy],
                            send_sem=s1, recv_sem=r1, **device(zi * PER_Z + batch, ys[dy]),
                        )
                        if dc or dy:
                            copy.start()
                        else:
                            pl.when(step < 3)(copy.start)

    pltpu.make_async_copy(recv1.at[pl.ds(1, GROUP - 1)], recv1.at[pl.ds(1, GROUP - 1)], r1).wait()
    own_sum = pieces[me]
    for d in range(1, GROUP):
        own_sum = own_sum + recv1[d]
    recv2[zi] = own_sum

    for dz in (4, 3, 5, 2, 6, 1, 7):
        pltpu.make_async_remote_copy(
            src_ref=recv2.at[zi], dst_ref=recv2.at[zi], send_sem=s2, recv_sem=r2,
            **device(zs[dz] * PER_Z + inz, fq),
        ).start()
    pltpu.make_async_copy(recv2.at[pl.ds(0, NZ - 1)], recv2.at[pl.ds(0, NZ - 1)], r2).wait()
    both = recv2[0]
    for z in range(1, NZ):
        both = both + recv2[z]
    both = both * (1.0 / (NB * math.sqrt(128 * 512)))

    c16 = jnp.concatenate([both, pltpu.roll(both, 64, 1)], axis=0)
    c16 = jnp.where(lane < 64, c16, 0.0)
    odd = (lane // 16) % 2 == 1
    mat = jnp.concatenate([jnp.where(odd, -c16, c16), swap16(c16, lane)], axis=0)
    turned = jnp.concatenate([mat, jnp.zeros((96, LANES), F32)], axis=0).T
    lane32 = lax.broadcasted_iota(jnp.int32, (32, LANES), 1)
    row32 = lax.broadcasted_iota(jnp.int32, (32, LANES), 0)
    lane1 = lax.broadcasted_iota(jnp.int32, (1, LANES), 1)
    mat_t = jnp.where(lane32 < 32, turned[0:32], pltpu.roll(turned[32:64], 32, 1))

    def by_triad(value, lanes):
        first = jnp.sum(jnp.where(lanes < 32, value, 0.0), axis=1, keepdims=True)
        second = jnp.sum(jnp.where((lanes >= 32) & (lanes < 64), value, 0.0), axis=1, keepdims=True)
        return jnp.where(lanes < 32, first, second)

    def to_lanes(vec):
        return jnp.sum(mat_t * vec, axis=0, keepdims=True)

    vec = jnp.where(row32 < 16, 1.0 / math.sqrt(NB), 0.0).astype(F32)
    for _ in range(POW // 2):
        out = to_lanes(vec)
        out = out / jnp.sqrt(by_triad(out * out, lane1))
        vec = by_triad(mat * out, lane32)
        vec = vec / jnp.sqrt(jnp.sum(vec * vec, axis=0, keepdims=True))
    out = to_lanes(vec)
    lead = jnp.where(lane1 < 64, jnp.sum(jnp.where(lane32 % 32 == row32, vec, 0.0), axis=0, keepdims=True), 0.0)
    val_re = by_triad(lead * out, lane1)
    crossed = lead * swap16(out, lane1)
    val_im = by_triad(jnp.where((lane1 // 16) % 2 == 0, crossed, -crossed), lane1)
    spot = lane1 - 2 * me
    re0, re1 = val_re[:, 0:1], val_re[:, 32:33]
    im0, im1 = val_im[:, 0:1], val_im[:, 32:33]
    vals = jnp.where(spot == 0, re0, jnp.where(spot == 1, re1, 0.0))
    vals = vals + jnp.where(spot == 64, im0, jnp.where(spot == 65, im1, 0.0))
    placed = jnp.where((me % 2) == 1, pltpu.roll(lead, 64, 1), lead)
    out3[...] = jnp.concatenate([placed, vals], axis=0)
    recv3[me] = out3[...]

    for dx, dc, dy in far_first:
        pltpu.make_async_remote_copy(
            src_ref=out3, dst_ref=recv3.at[me], send_sem=s3, recv_sem=r3, **device(plane_spaces[dx, dc], ys[dy])
        ).start()
    row_lhs = lax.broadcasted_iota(jnp.int32, (16, 2 * LANES), 0)
    lane_lhs = lax.broadcasted_iota(jnp.int32, (16, 2 * LANES), 1)
    live = lane_lhs // 32 == row_lhs // 2
    pltpu.make_async_copy(recv3.at[pl.ds(0, GROUP - 1)], recv3.at[pl.ds(0, GROUP - 1)], r3).wait()

    vals_all = recv3[0][1:2]
    for q in range(1, GROUP):
        vals_all = vals_all + recv3[q][1:2]
    vals_ref[...] = jnp.concatenate([vals_all, pltpu.roll(vals_all, 64, 1)], axis=0)[:, 0:NTRI]

    @pl.loop(0, NBATCH // 2)
    def _(pair):
        for k in (0, 1):
            batch = 2 * pair + k
            parts = [recv3[4 * batch + 2 * h][0:1] + recv3[4 * batch + 2 * h + 1][0:1] for h in (0, 1)]
            flat = jnp.concatenate([jnp.where((lane1 // 16) % 2 == 1, -p, p) for p in parts], axis=1)
            turned = jnp.concatenate([swap16(p, lane1) for p in parts], axis=1)
            coeff = jnp.where(live, jnp.where(row_lhs % 2 == 0, flat, turned), 0.0)
            high, low = split(coeff)
            stacked = jnp.concatenate([high, low], axis=0)
            fields = jnp.concatenate([rhi[0, batch, :, 0:LANES], rhi[1, batch, :, 0:LANES]], axis=1)
            res = dot_nn(stacked, fields)
            res = res[0:16] + res[16:32]
            modes_ref[pl.ds(batch * 32 + x_fast, 16, stride=2), :] = res[:, 0:LANES]
            modes_ref[pl.ds(batch * 32 + x_slow, 16, stride=2), :] = res[:, LANES:]

    pltpu.make_async_copy(recv1.at[pl.ds(1, GROUP - 1)], recv1.at[pl.ds(1, GROUP - 1)], s1).wait()
    pltpu.make_async_copy(recv2.at[pl.ds(0, NZ - 1)], recv2.at[pl.ds(0, NZ - 1)], s2).wait()
    pltpu.make_async_copy(recv3.at[pl.ds(0, GROUP - 1)], recv3.at[pl.ds(0, GROUP - 1)], s3).wait()


def on_device(u_velocity, v_velocity, cell_weights, block_offsets, triads):
    transform, hann, small = tables()
    u_rows = u_velocity.reshape(2 * NT, LANES)
    v_rows = v_velocity.reshape(2 * NT, LANES)
    anywhere = pl.BlockSpec(memory_space=pltpu.HBM)
    vmem = pl.BlockSpec(memory_space=pltpu.VMEM)
    smem = pl.BlockSpec(memory_space=pltpu.SMEM)
    dma = pltpu.SemaphoreType.DMA
    fields, values = pl.pallas_call(
        kernel,
        out_shape=(jax.ShapeDtypeStruct((4 * NTRI, LANES), F32), jax.ShapeDtypeStruct((2, NTRI), F32)),
        in_specs=[anywhere] * 5 + [vmem, smem, smem],
        out_specs=(vmem, vmem),
        scratch_shapes=[
            pltpu.VMEM((2 * NT, LANES), BF16),
            pltpu.VMEM((2 * NT, LANES), BF16),
            pltpu.VMEM((NFFT, NFFT), BF16),
            pltpu.VMEM((NFFT, LANES), F32),
            pltpu.VMEM((160, LANES), BF16),
            pltpu.VMEM((2 * NT, LANES), F32),
            pltpu.VMEM((2 * NT, LANES), F32),
            pltpu.VMEM((2, NT, LANES), BF16),
            pltpu.VMEM((2, NT, LANES), BF16),
            pltpu.VMEM((2, 1, 2 * NT), F32),
            pltpu.VMEM((2, 1, 2 * NT), F32),
            pltpu.VMEM((2, NT, LANES), F32),
            pltpu.VMEM((2, NFFT * NB, LANES), F32),
            pltpu.VMEM((2, 2 * BATCH * NB, 2 * LANES), BF16),
            pltpu.VMEM((2, NBATCH, 2 * BATCH * NB, 2 * LANES), BF16),
            pltpu.VMEM((2, 2 * BATCH * NB, 2 * LANES), BF16),
            pltpu.VMEM((2 * NBATCH, NB, LANES), F32),
            pltpu.VMEM((GROUP, 8, LANES), F32),
            pltpu.VMEM((GROUP, 8, LANES), F32),
            pltpu.VMEM((NZ, 8, LANES), F32),
            pltpu.VMEM((GROUP, 2, LANES), F32),
            pltpu.VMEM((2, LANES), F32),
            dma((8,)),
            dma((2, 4)), dma((2, 4)), dma((2,)), dma((2,)),
            dma(()), dma(()), dma(()), dma(()), dma(()), dma(()),
        ],
        compiler_params=pltpu.CompilerParams(
            collective_id=0, has_side_effects=True, vmem_limit_bytes=48 * 1024 * 1024
        ),
        name="bispectrum",
    )(
        *[
            pltpu.with_memory_space_constraint(array, pltpu.HBM)
            for array in (u_rows, v_rows, transform, hann, small, cell_weights, block_offsets, triads.T)
        ]
    )
    return values.T, fields.reshape(NTRI, 2, 2, LANES)


def solution(mesh):
    return jax.shard_map(
        on_device,
        mesh=mesh,
        in_specs=(P(None, "space", "freq"), P(None, "space", "freq"), P("space", "freq"), P(), P()),
        out_specs=(P(), P(None, None, "space", "freq")),
        check_vma=False,
    )
```

```python
import math

import jax
import jax.numpy as jnp
import numpy as np
from jax import lax
from jax.experimental import pallas as pl
from jax.experimental.pallas import tpu as pltpu
from jax.sharding import PartitionSpec as P

NFFT = 256
HALF = NFFT // 2
NB = 16
PITCH = 17
POW = 4
NT = 2176
LANES = 128
NTRI = 64
NZ = 8
GROUP = 32
PER_Z = 8
NFREQ = 4
BATCH = 8
NBATCH = NTRI // BATCH
SUB = 64
CHUNKS = ((0, 256), (256, 448), (704, 704), (1408, 768))
F32 = jnp.float32
BF16 = jnp.bfloat16


def tables():
    times = np.arange(NFFT)
    freqs = np.arange(HALF)
    angles = (freqs[:, None] * times[None, :] % NFFT).astype(np.float32) * np.float32(2.0 * math.pi / NFFT)
    window = (0.5 - 0.5 * np.cos(times * (2.0 * math.pi / NFFT))).astype(np.float32)
    scaling = np.float32(1.0 / np.sqrt(np.sum(window.astype(np.float64) ** 2)))
    transform = np.concatenate(
        [np.cos(angles.astype(np.float64)) * scaling, -np.sin(angles.astype(np.float64)) * scaling], axis=0
    )
    hann = np.ascontiguousarray(np.broadcast_to(window[:, None], (NFFT, LANES)))
    return transform.astype(jnp.bfloat16), hann


def dot_nt(lhs, rhs):
    return lax.dot_general(lhs, rhs, (((1,), (1,)), ((), ())), preferred_element_type=F32)


def dot_nn(lhs, rhs):
    return lax.dot_general(lhs, rhs, (((1,), (0,)), ((), ())), preferred_element_type=F32)


def split(value):
    high = value.astype(BF16)
    return high, (value - high.astype(F32)).astype(BF16)


def swap16(value, lane):
    return jnp.where(
        (lane // 16) % 2 == 0, pltpu.roll(value, LANES - 16, value.ndim - 1), pltpu.roll(value, 16, value.ndim - 1)
    )


def kernel(
    u_hbm, v_hbm, table_hbm, hann_hbm, w_ref, offs, tri,
    modes_ref, vals_ref,
    ubuf, vbuf, table, hann, vf, duf, snd, halo, colsend, colrecv, vort, spec,
    lhs, rhi, rlo, cross, pieces, recv1, recv2, recv3, out3,
    load_sem, vsend, vrecv, usend, urecv, s1, r1, s2, r2, s3, r3,
):
    sp = lax.axis_index("space")
    fq = lax.axis_index("freq")
    core = sp % 2
    zi = sp // PER_Z
    xi = (sp // 2) % 4
    inz = sp % PER_Z
    me = inz * NFREQ + fq
    sibling = sp + 1 - 2 * core
    outer = (sp + 63 + 2 * core) % 64
    cores = [core, 1 - core]
    xs = [xi] + [(xi + d) % 4 for d in (1, 2, 3)]
    ys = [fq] + [(fq + d) % NFREQ for d in (1, 2, 3)]
    zs = [zi] + [(zi + d) % NZ for d in range(1, NZ)]
    x_slow = core
    x_fast = 1 - core
    sign = (1 - 2 * core).astype(F32)

    def device(space, freq):
        return {"device_id": {"space": space, "freq": freq}, "device_id_type": pl.DeviceIdType.MESH}

    loads_v = []
    for n, (t0, cnt) in enumerate(CHUNKS):
        rows = pl.ds(2 * t0, 2 * cnt)
        loads_v.append(pltpu.make_async_copy(v_hbm.at[rows], vbuf.at[rows], load_sem.at[n]))
    load_u = pltpu.make_async_copy(u_hbm, ubuf, load_sem.at[4])
    load_h = pltpu.make_async_copy(hann_hbm, hann, load_sem.at[6])
    load_t = pltpu.make_async_copy(table_hbm, table, load_sem.at[7])
    loads_v[0].start()
    load_u.start()
    for load in loads_v[1:]:
        load.start()
    load_h.start()
    load_t.start()

    barrier = pltpu.get_barrier_semaphore()
    pl.semaphore_signal(barrier, inc=1, **device(outer, fq))
    for dz in (4, 3, 5, 2, 6, 1, 7):
        pl.semaphore_signal(barrier, inc=1, **device(zs[dz] * PER_Z + inz, fq))
    plane_spaces = {(dx, dc): zi * PER_Z + xs[dx] * 2 + cores[dc] for dx in range(4) for dc in (0, 1)}
    far_first = sorted(
        ((dx, dc, dy) for dx in range(4) for dc in (0, 1) for dy in range(4) if dx or dc or dy),
        key=lambda step: -(min(step[0], 4 - step[0]) + min(step[2], 4 - step[2])),
    )
    for dx, dc, dy in far_first:
        pl.semaphore_signal(barrier, inc=1, **device(plane_spaces[dx, dc], ys[dy]))

    def unpack(n):
        t0, cnt = CHUNKS[n]
        loads_v[n].wait()

        @pl.loop(t0 // SUB, (t0 + cnt) // SUB)
        def _(i):
            both = pl.ds(pl.multiple_of(i * 2 * SUB, 2 * SUB), 2 * SUB)
            one = pl.ds(pl.multiple_of(i * SUB, SUB), SUB)
            vf[both, :] = vbuf[both, :].astype(F32)
            snd[1, one, :] = vf[pl.ds(i * 2 * SUB + x_slow, SUB, stride=2), :].astype(BF16)
            snd[0, one, :] = vf[pl.ds(i * 2 * SUB + x_fast, SUB, stride=2), :].astype(BF16)

    copies_v = {}

    def send(n, plane, target):
        rows = pl.ds(CHUNKS[n][0], CHUNKS[n][1])
        copies_v[n, plane] = pltpu.make_async_remote_copy(
            src_ref=snd.at[plane, rows], dst_ref=halo.at[plane, rows],
            send_sem=vsend.at[plane, n], recv_sem=vrecv.at[plane, n], **device(target, fq),
        )
        copies_v[n, plane].start()

    unpack(0)
    pl.semaphore_wait(barrier, GROUP - 1 + NZ - 1 + 1)
    send(0, 1, outer)
    send(0, 0, sibling)
    unpack(1)
    send(1, 1, outer)
    send(1, 0, sibling)
    load_u.wait()
    lane8 = lax.broadcasted_iota(jnp.int32, (8, LANES), 1)
    at_edge = (lane8 == 0) | (lane8 == LANES - 1)

    @pl.loop(0, 2 * NT // 256)
    def _(g):
        block = ubuf[pl.ds(pl.multiple_of(g * 256, 256), 256), :].astype(F32)
        packed = jnp.zeros((8, LANES), F32)
        for i in range(32):
            packed = packed + pltpu.roll(jnp.where(at_edge, block[8 * i:8 * i + 8], 0.0), 2 * i + 1, 1)
        colsend[g] = packed.astype(BF16)

    copies_u = []
    for slot, target in ((1, ys[3]), (0, ys[1])):
        copies_u.append(
            pltpu.make_async_remote_copy(
                src_ref=colsend, dst_ref=colrecv.at[slot],
                send_sem=usend.at[slot], recv_sem=urecv.at[slot], **device(sp, target),
            )
        )
        copies_u[-1].start()
    for n in range(2, len(CHUNKS)):
        unpack(n)
        send(n, 1, outer)
        send(n, 0, sibling)

    has_left = (fq > 0).astype(F32)
    has_right = (fq < NFREQ - 1).astype(F32)
    for copy in copies_u:
        copy.wait()

    @pl.loop(0, 2 * NT // 256)
    def _(g):
        from_left = pltpu.roll(colrecv[0, g].astype(F32) * has_left, 1, 1)
        from_right = pltpu.roll(colrecv[1, g].astype(F32) * has_right, LANES - 1, 1)
        packed = jnp.where(lane8 % 2 == 0, from_right, from_left)
        rows = pl.ds(pl.multiple_of(g * 256, 256), 256)
        block = ubuf[rows, :].astype(F32)
        parts = []
        for i in range(32):
            value = block[8 * i:8 * i + 8]
            edge = pltpu.roll(packed, LANES - 1 - 2 * i, 1)
            after = jnp.where(lane8 == LANES - 1, edge, pltpu.roll(value, LANES - 1, 1))
            before = jnp.where(lane8 == 0, edge, pltpu.roll(value, 1, 1))
            parts.append(0.5 * (after - before))
        duf[rows, :] = jnp.concatenate(parts, axis=0)

    load_h.wait()
    load_t.wait()
    lane = lax.broadcasted_iota(jnp.int32, (16, LANES), 1)
    quarter = lane // 32
    has_outer = jnp.where(core == 0, sp > 0, sp < 63).astype(F32)

    for plane in (0, 1):
        own = x_fast if plane == 0 else x_slow
        other = x_slow if plane == 0 else x_fast
        half = 0.5 * sign if plane == 0 else -0.5 * sign
        mask = 1.0 if plane == 0 else has_outer
        total = jnp.zeros((8, LANES), F32)
        for n, (t0, cnt) in enumerate(CHUNKS):
            copies_v[n, plane].wait()

            def vorticity(i, total):
                one = pl.ds(pl.multiple_of(i * SUB, SUB), SUB)
                far = halo[plane, one, :].astype(F32) * mask
                near = vf[pl.ds(i * 2 * SUB + other, SUB, stride=2), :]
                value = half * (far - near) - duf[pl.ds(i * 2 * SUB + own, SUB, stride=2), :]
                vort[plane, one, :] = value
                return total + jnp.sum(value.reshape(SUB // 8, 8, LANES), axis=0)

            total = lax.fori_loop(t0 // SUB, (t0 + cnt) // SUB, vorticity, total)
        mean = jnp.sum(total, axis=0, keepdims=True) * (1.0 / NT)

        @pl.loop(0, NB // 4, unroll=True)
        def _(four):
            for h in (0, 1):
                parts = []
                for k in (0, 1):
                    block = vort[plane, pl.ds(offs[4 * four + 2 * h + k], NFFT), :]
                    parts.append(((block - mean) * hann[...]).astype(BF16))
                out = dot_nn(table[...], jnp.concatenate(parts, axis=1))
                for k in (0, 1):
                    spec[plane, pl.ds(4 * four + 2 * h + k, NFFT, stride=PITCH), :] = out[:, k * LANES:(k + 1) * LANES]

        weight = w_ref[pl.ds(own, 1), :]

        @pl.loop(0, 4, unroll=True)
        def _(step):
            x_to = (xi + 3 - step) % 4
            for dc in (1, 0):
                batch = x_to * 2 + cores[dc]
                for i in range(BATCH):
                    j = batch * BATCH + i
                    k_at = tri[0, j]
                    l_at = tri[1, j]

                    def rows_of(f):
                        return spec[plane, pl.ds(f * PITCH, NB), :]

                    k_re, k_im = rows_of(k_at), rows_of(k_at + HALF)
                    l_re, l_im = rows_of(l_at), rows_of(l_at + HALF)
                    t_re, t_im = rows_of(k_at + l_at), rows_of(k_at + l_at + HALF)
                    p_re = (k_re * l_re - k_im * l_im) * weight
                    p_im = (k_re * l_im + k_im * l_re) * weight
                    for c, value in ((0, p_re), (1, p_im)):
                        high, low = split(value)
                        lhs[dc, i * NB:(i + 1) * NB, c * LANES:(c + 1) * LANES] = high
                        lhs[dc, 128 + i * NB:128 + (i + 1) * NB, c * LANES:(c + 1) * LANES] = low
                    re_hi, re_lo = split(t_re)
                    im_hi, im_lo = split(t_im)
                    at_re = slice(2 * i * NB, (2 * i + 1) * NB)
                    at_im = slice((2 * i + 1) * NB, (2 * i + 2) * NB)
                    rhi[plane, batch, at_re, 0:LANES] = re_hi
                    rhi[plane, batch, at_im, 0:LANES] = im_hi
                    rhi[plane, batch, at_re, LANES:] = im_hi
                    rhi[plane, batch, at_im, LANES:] = -re_hi
                    rlo[dc, at_re, 0:LANES] = re_lo
                    rlo[dc, at_im, 0:LANES] = im_lo
                    rlo[dc, at_re, LANES:] = im_lo
                    rlo[dc, at_im, LANES:] = -re_lo
                out = dot_nt(lhs[dc], rhi[plane, batch])
                out = out[0:128] + out[128:256] + dot_nt(lhs[dc, 0:128], rlo[dc])
                for h in (0, 1):
                    cols = slice(h * LANES, (h + 1) * LANES)
                    acc = out[h * 64:h * 64 + 16, cols]
                    for i in (1, 2, 3):
                        acc = jnp.where(quarter == i, out[h * 64 + i * 16:h * 64 + i * 16 + 16, cols], acc)
                    if plane == 0:
                        cross[2 * batch + h] = acc
                    else:
                        acc = acc + cross[2 * batch + h]
                        low, high = acc[0:8], acc[8:16]
                        first = lane[0:8] < 64
                        pieces[4 * batch + 2 * h] = jnp.where(first, low, pltpu.roll(high, 64, 1))
                        pieces[4 * batch + 2 * h + 1] = jnp.where(first, pltpu.roll(low, 64, 1), high)
                if plane == 1:
                    for dy in (2, 1, 3, 0):
                        copy = pltpu.make_async_remote_copy(
                            src_ref=pieces.at[4 * batch + ys[dy]], dst_ref=recv1.at[(3 - step) * 8 + dc * 4 + dy],
                            send_sem=s1, recv_sem=r1, **device(zi * PER_Z + batch, ys[dy]),
                        )
                        if dc or dy:
                            copy.start()
                        else:
                            pl.when(step < 3)(copy.start)

    pltpu.make_async_copy(recv1.at[pl.ds(1, GROUP - 1)], recv1.at[pl.ds(1, GROUP - 1)], r1).wait()
    own_sum = pieces[me]
    for d in range(1, GROUP):
        own_sum = own_sum + recv1[d]
    recv2[zi] = own_sum

    for dz in (4, 3, 5, 2, 6, 1, 7):
        pltpu.make_async_remote_copy(
            src_ref=recv2.at[zi], dst_ref=recv2.at[zi], send_sem=s2, recv_sem=r2,
            **device(zs[dz] * PER_Z + inz, fq),
        ).start()
    pltpu.make_async_copy(recv2.at[pl.ds(0, NZ - 1)], recv2.at[pl.ds(0, NZ - 1)], r2).wait()
    both = recv2[0]
    for z in range(1, NZ):
        both = both + recv2[z]
    both = both * (1.0 / (NB * math.sqrt(128 * 512)))

    c16 = jnp.concatenate([both, pltpu.roll(both, 64, 1)], axis=0)
    c16 = jnp.where(lane < 64, c16, 0.0)
    odd = (lane // 16) % 2 == 1
    mat = jnp.concatenate([jnp.where(odd, -c16, c16), swap16(c16, lane)], axis=0)
    turned = jnp.concatenate([mat, jnp.zeros((96, LANES), F32)], axis=0).T
    lane32 = lax.broadcasted_iota(jnp.int32, (32, LANES), 1)
    row32 = lax.broadcasted_iota(jnp.int32, (32, LANES), 0)
    lane1 = lax.broadcasted_iota(jnp.int32, (1, LANES), 1)
    mat_t = jnp.where(lane32 < 32, turned[0:32], pltpu.roll(turned[32:64], 32, 1))

    def by_triad(value, lanes):
        first = jnp.sum(jnp.where(lanes < 32, value, 0.0), axis=1, keepdims=True)
        second = jnp.sum(jnp.where((lanes >= 32) & (lanes < 64), value, 0.0), axis=1, keepdims=True)
        return jnp.where(lanes < 32, first, second)

    def to_lanes(vec):
        return jnp.sum(mat_t * vec, axis=0, keepdims=True)

    vec = jnp.where(row32 < 16, 1.0 / math.sqrt(NB), 0.0).astype(F32)
    for _ in range(POW // 2):
        out = to_lanes(vec)
        out = out / jnp.sqrt(by_triad(out * out, lane1))
        vec = by_triad(mat * out, lane32)
        vec = vec / jnp.sqrt(jnp.sum(vec * vec, axis=0, keepdims=True))
    out = to_lanes(vec)
    lead = jnp.where(lane1 < 64, jnp.sum(jnp.where(lane32 % 32 == row32, vec, 0.0), axis=0, keepdims=True), 0.0)
    val_re = by_triad(lead * out, lane1)
    crossed = lead * swap16(out, lane1)
    val_im = by_triad(jnp.where((lane1 // 16) % 2 == 0, crossed, -crossed), lane1)
    spot = lane1 - 2 * me
    re0, re1 = val_re[:, 0:1], val_re[:, 32:33]
    im0, im1 = val_im[:, 0:1], val_im[:, 32:33]
    vals = jnp.where(spot == 0, re0, jnp.where(spot == 1, re1, 0.0))
    vals = vals + jnp.where(spot == 64, im0, jnp.where(spot == 65, im1, 0.0))
    placed = jnp.where((me % 2) == 1, pltpu.roll(lead, 64, 1), lead)
    out3[...] = jnp.concatenate([placed, vals], axis=0)
    recv3[me] = out3[...]

    for dx, dc, dy in far_first:
        pltpu.make_async_remote_copy(
            src_ref=out3, dst_ref=recv3.at[me], send_sem=s3, recv_sem=r3, **device(plane_spaces[dx, dc], ys[dy])
        ).start()
    row_lhs = lax.broadcasted_iota(jnp.int32, (16, 2 * LANES), 0)
    lane_lhs = lax.broadcasted_iota(jnp.int32, (16, 2 * LANES), 1)
    live = lane_lhs // 32 == row_lhs // 2
    pltpu.make_async_copy(recv3.at[pl.ds(0, GROUP - 1)], recv3.at[pl.ds(0, GROUP - 1)], r3).wait()

    vals_all = recv3[0][1:2]
    for q in range(1, GROUP):
        vals_all = vals_all + recv3[q][1:2]
    vals_ref[...] = jnp.concatenate([vals_all, pltpu.roll(vals_all, 64, 1)], axis=0)[:, 0:NTRI]

    @pl.loop(0, NBATCH // 2, unroll=True)
    def _(pair):
        for k in (0, 1):
            batch = 2 * pair + k
            parts = [recv3[4 * batch + 2 * h][0:1] + recv3[4 * batch + 2 * h + 1][0:1] for h in (0, 1)]
            flat = jnp.concatenate([jnp.where((lane1 // 16) % 2 == 1, -p, p) for p in parts], axis=1)
            turned = jnp.concatenate([swap16(p, lane1) for p in parts], axis=1)
            coeff = jnp.where(live, jnp.where(row_lhs % 2 == 0, flat, turned), 0.0)
            high, low = split(coeff)
            stacked = jnp.concatenate([high, low], axis=0)
            fields = jnp.concatenate([rhi[0, batch, :, 0:LANES], rhi[1, batch, :, 0:LANES]], axis=1)
            res = dot_nn(stacked, fields)
            res = res[0:16] + res[16:32]
            modes_ref[pl.ds(batch * 32 + x_fast, 16, stride=2), :] = res[:, 0:LANES]
            modes_ref[pl.ds(batch * 32 + x_slow, 16, stride=2), :] = res[:, LANES:]

    pltpu.make_async_copy(recv1.at[pl.ds(1, GROUP - 1)], recv1.at[pl.ds(1, GROUP - 1)], s1).wait()
    pltpu.make_async_copy(recv2.at[pl.ds(0, NZ - 1)], recv2.at[pl.ds(0, NZ - 1)], s2).wait()
    pltpu.make_async_copy(recv3.at[pl.ds(0, GROUP - 1)], recv3.at[pl.ds(0, GROUP - 1)], s3).wait()


def on_device(u_velocity, v_velocity, cell_weights, block_offsets, triads):
    transform, hann = tables()
    u_rows = u_velocity.reshape(2 * NT, LANES)
    v_rows = v_velocity.reshape(2 * NT, LANES)
    anywhere = pl.BlockSpec(memory_space=pltpu.HBM)
    vmem = pl.BlockSpec(memory_space=pltpu.VMEM)
    smem = pl.BlockSpec(memory_space=pltpu.SMEM)
    dma = pltpu.SemaphoreType.DMA
    fields, values = pl.pallas_call(
        kernel,
        out_shape=(jax.ShapeDtypeStruct((4 * NTRI, LANES), F32), jax.ShapeDtypeStruct((2, NTRI), F32)),
        in_specs=[anywhere] * 4 + [vmem, smem, smem],
        out_specs=(vmem, vmem),
        scratch_shapes=[
            pltpu.VMEM((2 * NT, LANES), BF16),
            pltpu.VMEM((2 * NT, LANES), BF16),
            pltpu.VMEM((NFFT, NFFT), BF16),
            pltpu.VMEM((NFFT, LANES), F32),
            pltpu.VMEM((2 * NT, LANES), F32),
            pltpu.VMEM((2 * NT, LANES), F32),
            pltpu.VMEM((2, NT, LANES), BF16),
            pltpu.VMEM((2, NT, LANES), BF16),
            pltpu.VMEM((2 * NT // 256, 8, LANES), BF16),
            pltpu.VMEM((2, 2 * NT // 256, 8, LANES), BF16),
            pltpu.VMEM((2, NT, LANES), F32),
            pltpu.VMEM((2, NFFT * PITCH, LANES), F32),
            pltpu.VMEM((2, 2 * BATCH * NB, 2 * LANES), BF16),
            pltpu.VMEM((2, NBATCH, 2 * BATCH * NB, 2 * LANES), BF16),
            pltpu.VMEM((2, 2 * BATCH * NB, 2 * LANES), BF16),
            pltpu.VMEM((2 * NBATCH, NB, LANES), F32),
            pltpu.VMEM((GROUP, 8, LANES), F32),
            pltpu.VMEM((GROUP, 8, LANES), F32),
            pltpu.VMEM((NZ, 8, LANES), F32),
            pltpu.VMEM((GROUP, 2, LANES), F32),
            pltpu.VMEM((2, LANES), F32),
            dma((8,)),
            dma((2, 4)), dma((2, 4)), dma((2,)), dma((2,)),
            dma(()), dma(()), dma(()), dma(()), dma(()), dma(()),
        ],
        compiler_params=pltpu.CompilerParams(
            collective_id=0, has_side_effects=True, vmem_limit_bytes=48 * 1024 * 1024
        ),
        name="bispectrum",
    )(
        *[
            pltpu.with_memory_space_constraint(array, pltpu.HBM)
            for array in (u_rows, v_rows, transform, hann, cell_weights, block_offsets, triads.T)
        ]
    )
    return values.T, fields.reshape(NTRI, 2, 2, LANES)


def solution(mesh):
    return jax.shard_map(
        on_device,
        mesh=mesh,
        in_specs=(P(None, "space", "freq"), P(None, "space", "freq"), P("space", "freq"), P(), P()),
        out_specs=(P(), P(None, None, "space", "freq")),
        check_vma=False,
    )
```

```python
import math

import jax
import jax.numpy as jnp
import numpy as np
from jax import lax
from jax.experimental import pallas as pl
from jax.experimental.pallas import tpu as pltpu
from jax.sharding import PartitionSpec as P

NFFT = 256
HALF = NFFT // 2
NB = 16
PITCH = 17
POW = 4
NT = 2176
LANES = 128
NTRI = 64
NZ = 8
GROUP = 32
PER_Z = 8
NFREQ = 4
BATCH = 8
NBATCH = NTRI // BATCH
SUB = 64
CHUNKS = ((0, 320), (320, 448), (768, 640), (1408, 768))
F32 = jnp.float32
BF16 = jnp.bfloat16


def tables():
    times = np.arange(NFFT)
    freqs = np.arange(HALF)
    angles = (freqs[:, None] * times[None, :] % NFFT).astype(np.float32) * np.float32(2.0 * math.pi / NFFT)
    window = (0.5 - 0.5 * np.cos(times * (2.0 * math.pi / NFFT))).astype(np.float32)
    scaling = np.float32(1.0 / np.sqrt(np.sum(window.astype(np.float64) ** 2)))
    transform = np.concatenate(
        [np.cos(angles.astype(np.float64)) * scaling, -np.sin(angles.astype(np.float64)) * scaling], axis=0
    )
    hann = np.ascontiguousarray(np.broadcast_to(window[:, None], (NFFT, LANES)))
    return transform.astype(jnp.bfloat16), hann


def dot_nt(lhs, rhs):
    return lax.dot_general(lhs, rhs, (((1,), (1,)), ((), ())), preferred_element_type=F32)


def dot_nn(lhs, rhs):
    return lax.dot_general(lhs, rhs, (((1,), (0,)), ((), ())), preferred_element_type=F32)


def split(value):
    high = value.astype(BF16)
    return high, (value - high.astype(F32)).astype(BF16)


def swap16(value, lane):
    return jnp.where(
        (lane // 16) % 2 == 0, pltpu.roll(value, LANES - 16, value.ndim - 1), pltpu.roll(value, 16, value.ndim - 1)
    )


def kernel(
    u_hbm, v_hbm, table_hbm, hann_hbm, w_ref, offs, tri,
    modes_ref, vals_ref,
    ubuf, vbuf, table, hann, vf, duf, snd, halo, colsend, colrecv, vort, spec,
    lhs, rhi, rlo, cross, pieces, recv1, recv2, recv3, out3,
    load_sem, vsend, vrecv, usend, urecv, s1, r1, s2, r2, s3, r3,
):
    sp = lax.axis_index("space")
    fq = lax.axis_index("freq")
    core = sp % 2
    zi = sp // PER_Z
    xi = (sp // 2) % 4
    inz = sp % PER_Z
    me = inz * NFREQ + fq
    sibling = sp + 1 - 2 * core
    outer = (sp + 63 + 2 * core) % 64
    cores = [core, 1 - core]
    xs = [xi] + [(xi + d) % 4 for d in (1, 2, 3)]
    ys = [fq] + [(fq + d) % NFREQ for d in (1, 2, 3)]
    zs = [zi] + [(zi + d) % NZ for d in range(1, NZ)]
    x_slow = core
    x_fast = 1 - core
    sign = (1 - 2 * core).astype(F32)

    def device(space, freq):
        return {"device_id": {"space": space, "freq": freq}, "device_id_type": pl.DeviceIdType.MESH}

    loads_v = []
    for n, (t0, cnt) in enumerate(CHUNKS):
        rows = pl.ds(2 * t0, 2 * cnt)
        loads_v.append(pltpu.make_async_copy(v_hbm.at[rows], vbuf.at[rows], load_sem.at[n]))
    load_u = pltpu.make_async_copy(u_hbm, ubuf, load_sem.at[4])
    load_h = pltpu.make_async_copy(hann_hbm, hann, load_sem.at[6])
    load_t = pltpu.make_async_copy(table_hbm, table, load_sem.at[7])
    loads_v[0].start()
    load_u.start()
    for load in loads_v[1:]:
        load.start()
    load_h.start()
    load_t.start()

    barrier = pltpu.get_barrier_semaphore()
    pl.semaphore_signal(barrier, inc=1, **device(outer, fq))
    for dz in (4, 3, 5, 2, 6, 1, 7):
        pl.semaphore_signal(barrier, inc=1, **device(zs[dz] * PER_Z + inz, fq))
    plane_spaces = {(dx, dc): zi * PER_Z + xs[dx] * 2 + cores[dc] for dx in range(4) for dc in (0, 1)}
    far_first = sorted(
        ((dx, dc, dy) for dx in range(4) for dc in (0, 1) for dy in range(4) if dx or dc or dy),
        key=lambda step: -(min(step[0], 4 - step[0]) + min(step[2], 4 - step[2])),
    )
    for dx, dc, dy in far_first:
        pl.semaphore_signal(barrier, inc=1, **device(plane_spaces[dx, dc], ys[dy]))

    def unpack(n):
        t0, cnt = CHUNKS[n]
        loads_v[n].wait()

        @pl.loop(t0 // SUB, (t0 + cnt) // SUB)
        def _(i):
            both = pl.ds(pl.multiple_of(i * 2 * SUB, 2 * SUB), 2 * SUB)
            one = pl.ds(pl.multiple_of(i * SUB, SUB), SUB)
            vf[both, :] = vbuf[both, :].astype(F32)
            snd[1, one, :] = vf[pl.ds(i * 2 * SUB + x_slow, SUB, stride=2), :].astype(BF16)
            snd[0, one, :] = vf[pl.ds(i * 2 * SUB + x_fast, SUB, stride=2), :].astype(BF16)

    copies_v = {}

    def send(n, plane, target):
        rows = pl.ds(CHUNKS[n][0], CHUNKS[n][1])
        copies_v[n, plane] = pltpu.make_async_remote_copy(
            src_ref=snd.at[plane, rows], dst_ref=halo.at[plane, rows],
            send_sem=vsend.at[plane, n], recv_sem=vrecv.at[plane, n], **device(target, fq),
        )
        copies_v[n, plane].start()

    lane8 = lax.broadcasted_iota(jnp.int32, (8, LANES), 1)
    pair8 = lane8 // 2
    rowm = lax.broadcasted_iota(jnp.int32, (LANES, LANES), 0)
    lanem = lax.broadcasted_iota(jnp.int32, (LANES, LANES), 1)
    pick = jnp.where(rowm == jnp.where(lanem % 2 == 0, LANES - 1, 0), 1.0, 0.0).astype(BF16)
    diff = jnp.where(rowm == lanem + 1, 0.5, jnp.where(rowm == lanem - 1, -0.5, 0.0)).astype(BF16)
    place = jnp.where(rowm % 2 == 0, jnp.where(lanem == 0, -0.5, 0.0), jnp.where(lanem == LANES - 1, 0.5, 0.0))
    diff = jnp.concatenate([diff, place.astype(BF16)], axis=0)

    unpack(0)
    pl.semaphore_wait(barrier, GROUP - 1 + NZ - 1 + 1)
    send(0, 1, outer)
    send(0, 0, sibling)
    load_u.wait()

    @pl.loop(0, 2 * NT // 256, unroll=True)
    def _(g):
        spread = dot_nn(ubuf[pl.ds(pl.multiple_of(g * 256, 256), 256), :], pick)
        packed = jnp.zeros((8, LANES), F32)
        for i in range(32):
            packed = jnp.where(pair8 == i, spread[8 * i:8 * i + 8], packed)
        colsend[g] = packed.astype(BF16)

    copies_u = []
    for slot, target in ((1, ys[3]), (0, ys[1])):
        copies_u.append(
            pltpu.make_async_remote_copy(
                src_ref=colsend, dst_ref=colrecv.at[slot],
                send_sem=usend.at[slot], recv_sem=urecv.at[slot], **device(sp, target),
            )
        )
        copies_u[-1].start()
    for n in range(1, len(CHUNKS)):
        unpack(n)
        send(n, 1, outer)
        send(n, 0, sibling)

    has_left = (fq > 0).astype(F32)
    has_right = (fq < NFREQ - 1).astype(F32)
    for copy in copies_u:
        copy.wait()

    @pl.loop(0, 2 * NT // 256, unroll=True)
    def _(g):
        from_left = colrecv[0, g].astype(F32) * has_left
        from_right = colrecv[1, g].astype(F32) * has_right
        packed = jnp.where(lane8 % 2 == 0, from_left, from_right)
        edges = jnp.concatenate([jnp.where(pair8 == i, packed, 0.0) for i in range(32)], axis=0).astype(BF16)
        rows = pl.ds(pl.multiple_of(g * 256, 256), 256)
        duf[rows, :] = dot_nn(jnp.concatenate([ubuf[rows, :], edges], axis=1), diff)

    load_h.wait()
    load_t.wait()
    lane = lax.broadcasted_iota(jnp.int32, (16, LANES), 1)
    quarter = lane // 32
    has_outer = jnp.where(core == 0, sp > 0, sp < 63).astype(F32)

    for plane in (0, 1):
        own = x_fast if plane == 0 else x_slow
        half = 0.5 * sign if plane == 0 else -0.5 * sign
        mask = 1.0 if plane == 0 else has_outer
        total = jnp.zeros((8, LANES), F32)
        for n, (t0, cnt) in enumerate(CHUNKS):
            copies_v[n, plane].wait()

            def vorticity(i, total):
                one = pl.ds(pl.multiple_of(i * SUB, SUB), SUB)
                far = halo[plane, one, :].astype(F32) * mask
                near = snd[1 - plane, one, :].astype(F32)
                value = half * (far - near) - duf[pl.ds(i * 2 * SUB + own, SUB, stride=2), :]
                vort[plane, one, :] = value
                return total + jnp.sum(value.reshape(SUB // 8, 8, LANES), axis=0)

            total = lax.fori_loop(t0 // SUB, (t0 + cnt) // SUB, vorticity, total, unroll=True)
        mean = jnp.sum(total, axis=0, keepdims=True) * (1.0 / NT)

        @pl.loop(0, NB // 4, unroll=True)
        def _(four):
            for h in (0, 1):
                parts = []
                for k in (0, 1):
                    block = vort[plane, pl.ds(offs[4 * four + 2 * h + k], NFFT), :]
                    parts.append(((block - mean) * hann[...]).astype(BF16))
                out = dot_nn(table[...], jnp.concatenate(parts, axis=1))
                for k in (0, 1):
                    spec[plane, pl.ds(4 * four + 2 * h + k, NFFT, stride=PITCH), :] = out[:, k * LANES:(k + 1) * LANES]

        weight = w_ref[pl.ds(own, 1), :]

        @pl.loop(0, 4, unroll=True)
        def _(step):
            x_to = (xi + 3 - step) % 4
            for dc in (1, 0):
                batch = x_to * 2 + cores[dc]
                for i in range(BATCH):
                    j = batch * BATCH + i
                    k_at = tri[0, j]
                    l_at = tri[1, j]

                    def rows_of(f):
                        return spec[plane, pl.ds(f * PITCH, NB), :]

                    k_re, k_im = rows_of(k_at), rows_of(k_at + HALF)
                    l_re, l_im = rows_of(l_at), rows_of(l_at + HALF)
                    t_re, t_im = rows_of(k_at + l_at), rows_of(k_at + l_at + HALF)
                    p_re = (k_re * l_re - k_im * l_im) * weight
                    p_im = (k_re * l_im + k_im * l_re) * weight
                    for c, value in ((0, p_re), (1, p_im)):
                        high, low = split(value)
                        lhs[dc, i * NB:(i + 1) * NB, c * LANES:(c + 1) * LANES] = high
                        lhs[dc, 128 + i * NB:128 + (i + 1) * NB, c * LANES:(c + 1) * LANES] = low
                    re_hi, re_lo = split(t_re)
                    im_hi, im_lo = split(t_im)
                    at_re = slice(2 * i * NB, (2 * i + 1) * NB)
                    at_im = slice((2 * i + 1) * NB, (2 * i + 2) * NB)
                    rhi[plane, batch, at_re, 0:LANES] = re_hi
                    rhi[plane, batch, at_im, 0:LANES] = im_hi
                    rhi[plane, batch, at_re, LANES:] = im_hi
                    rhi[plane, batch, at_im, LANES:] = -re_hi
                    rlo[dc, at_re, 0:LANES] = re_lo
                    rlo[dc, at_im, 0:LANES] = im_lo
                    rlo[dc, at_re, LANES:] = im_lo
                    rlo[dc, at_im, LANES:] = -re_lo
                out = dot_nt(lhs[dc], rhi[plane, batch])
                out = out[0:128] + out[128:256] + dot_nt(lhs[dc, 0:128], rlo[dc])
                for h in (0, 1):
                    cols = slice(h * LANES, (h + 1) * LANES)
                    acc = out[h * 64:h * 64 + 16, cols]
                    for i in (1, 2, 3):
                        acc = jnp.where(quarter == i, out[h * 64 + i * 16:h * 64 + i * 16 + 16, cols], acc)
                    if plane == 0:
                        cross[2 * batch + h] = acc
                    else:
                        acc = acc + cross[2 * batch + h]
                        low, high = acc[0:8], acc[8:16]
                        first = lane[0:8] < 64
                        pieces[4 * batch + 2 * h] = jnp.where(first, low, pltpu.roll(high, 64, 1))
                        pieces[4 * batch + 2 * h + 1] = jnp.where(first, pltpu.roll(low, 64, 1), high)
                if plane == 1:
                    for dy in (2, 1, 3, 0):
                        copy = pltpu.make_async_remote_copy(
                            src_ref=pieces.at[4 * batch + ys[dy]], dst_ref=recv1.at[(3 - step) * 8 + dc * 4 + dy],
                            send_sem=s1, recv_sem=r1, **device(zi * PER_Z + batch, ys[dy]),
                        )
                        if dc or dy:
                            copy.start()
                        else:
                            pl.when(step < 3)(copy.start)

    pltpu.make_async_copy(recv1.at[pl.ds(1, GROUP - 1)], recv1.at[pl.ds(1, GROUP - 1)], r1).wait()
    own_sum = pieces[me]
    for d in range(1, GROUP):
        own_sum = own_sum + recv1[d]
    recv2[zi] = own_sum

    for dz in (4, 3, 5, 2, 6, 1, 7):
        pltpu.make_async_remote_copy(
            src_ref=recv2.at[zi], dst_ref=recv2.at[zi], send_sem=s2, recv_sem=r2,
            **device(zs[dz] * PER_Z + inz, fq),
        ).start()
    pltpu.make_async_copy(recv2.at[pl.ds(0, NZ - 1)], recv2.at[pl.ds(0, NZ - 1)], r2).wait()
    both = recv2[0]
    for z in range(1, NZ):
        both = both + recv2[z]
    both = both * (1.0 / (NB * math.sqrt(128 * 512)))

    c16 = jnp.concatenate([both, pltpu.roll(both, 64, 1)], axis=0)
    c16 = jnp.where(lane < 64, c16, 0.0)
    odd = (lane // 16) % 2 == 1
    mat = jnp.concatenate([jnp.where(odd, -c16, c16), swap16(c16, lane)], axis=0)
    turned = jnp.concatenate([mat, jnp.zeros((96, LANES), F32)], axis=0).T
    lane32 = lax.broadcasted_iota(jnp.int32, (32, LANES), 1)
    row32 = lax.broadcasted_iota(jnp.int32, (32, LANES), 0)
    lane1 = lax.broadcasted_iota(jnp.int32, (1, LANES), 1)
    mat_t = jnp.where(lane32 < 32, turned[0:32], pltpu.roll(turned[32:64], 32, 1))

    def by_triad(value, lanes):
        first = jnp.sum(jnp.where(lanes < 32, value, 0.0), axis=1, keepdims=True)
        second = jnp.sum(jnp.where((lanes >= 32) & (lanes < 64), value, 0.0), axis=1, keepdims=True)
        return jnp.where(lanes < 32, first, second)

    def to_lanes(vec):
        return jnp.sum(mat_t * vec, axis=0, keepdims=True)

    vec = jnp.where(row32 < 16, 1.0 / math.sqrt(NB), 0.0).astype(F32)
    for _ in range(POW // 2):
        out = to_lanes(vec)
        out = out / jnp.sqrt(by_triad(out * out, lane1))
        vec = by_triad(mat * out, lane32)
        vec = vec / jnp.sqrt(jnp.sum(vec * vec, axis=0, keepdims=True))
    out = to_lanes(vec)
    lead = jnp.where(lane1 < 64, jnp.sum(jnp.where(lane32 % 32 == row32, vec, 0.0), axis=0, keepdims=True), 0.0)
    val_re = by_triad(lead * out, lane1)
    crossed = lead * swap16(out, lane1)
    val_im = by_triad(jnp.where((lane1 // 16) % 2 == 0, crossed, -crossed), lane1)
    spot = lane1 - 2 * me
    re0, re1 = val_re[:, 0:1], val_re[:, 32:33]
    im0, im1 = val_im[:, 0:1], val_im[:, 32:33]
    vals = jnp.where(spot == 0, re0, jnp.where(spot == 1, re1, 0.0))
    vals = vals + jnp.where(spot == 64, im0, jnp.where(spot == 65, im1, 0.0))
    placed = jnp.where((me % 2) == 1, pltpu.roll(lead, 64, 1), lead)
    out3[...] = jnp.concatenate([placed, vals], axis=0)
    recv3[me] = out3[...]

    for dx, dc, dy in far_first:
        pltpu.make_async_remote_copy(
            src_ref=out3, dst_ref=recv3.at[me], send_sem=s3, recv_sem=r3, **device(plane_spaces[dx, dc], ys[dy])
        ).start()
    row_lhs = lax.broadcasted_iota(jnp.int32, (16, 2 * LANES), 0)
    lane_lhs = lax.broadcasted_iota(jnp.int32, (16, 2 * LANES), 1)
    live = lane_lhs // 32 == row_lhs // 2
    pltpu.make_async_copy(recv3.at[pl.ds(0, GROUP - 1)], recv3.at[pl.ds(0, GROUP - 1)], r3).wait()

    vals_all = recv3[0][1:2]
    for q in range(1, GROUP):
        vals_all = vals_all + recv3[q][1:2]
    vals_ref[...] = jnp.concatenate([vals_all, pltpu.roll(vals_all, 64, 1)], axis=0)[:, 0:NTRI]

    @pl.loop(0, NBATCH // 2, unroll=True)
    def _(pair):
        for k in (0, 1):
            batch = 2 * pair + k
            parts = [recv3[4 * batch + 2 * h][0:1] + recv3[4 * batch + 2 * h + 1][0:1] for h in (0, 1)]
            flat = jnp.concatenate([jnp.where((lane1 // 16) % 2 == 1, -p, p) for p in parts], axis=1)
            turned = jnp.concatenate([swap16(p, lane1) for p in parts], axis=1)
            coeff = jnp.where(live, jnp.where(row_lhs % 2 == 0, flat, turned), 0.0)
            high, low = split(coeff)
            stacked = jnp.concatenate([high, low], axis=0)
            fields = jnp.concatenate([rhi[0, batch, :, 0:LANES], rhi[1, batch, :, 0:LANES]], axis=1)
            res = dot_nn(stacked, fields)
            res = res[0:16] + res[16:32]
            modes_ref[pl.ds(batch * 32 + x_fast, 16, stride=2), :] = res[:, 0:LANES]
            modes_ref[pl.ds(batch * 32 + x_slow, 16, stride=2), :] = res[:, LANES:]

    pltpu.make_async_copy(recv1.at[pl.ds(1, GROUP - 1)], recv1.at[pl.ds(1, GROUP - 1)], s1).wait()
    pltpu.make_async_copy(recv2.at[pl.ds(0, NZ - 1)], recv2.at[pl.ds(0, NZ - 1)], s2).wait()
    pltpu.make_async_copy(recv3.at[pl.ds(0, GROUP - 1)], recv3.at[pl.ds(0, GROUP - 1)], s3).wait()


def on_device(u_velocity, v_velocity, cell_weights, block_offsets, triads):
    transform, hann = tables()
    u_rows = u_velocity.reshape(2 * NT, LANES)
    v_rows = v_velocity.reshape(2 * NT, LANES)
    anywhere = pl.BlockSpec(memory_space=pltpu.HBM)
    vmem = pl.BlockSpec(memory_space=pltpu.VMEM)
    smem = pl.BlockSpec(memory_space=pltpu.SMEM)
    dma = pltpu.SemaphoreType.DMA
    fields, values = pl.pallas_call(
        kernel,
        out_shape=(jax.ShapeDtypeStruct((4 * NTRI, LANES), F32), jax.ShapeDtypeStruct((2, NTRI), F32)),
        in_specs=[anywhere] * 4 + [vmem, smem, smem],
        out_specs=(vmem, vmem),
        scratch_shapes=[
            pltpu.VMEM((2 * NT, LANES), BF16),
            pltpu.VMEM((2 * NT, LANES), BF16),
            pltpu.VMEM((NFFT, NFFT), BF16),
            pltpu.VMEM((NFFT, LANES), F32),
            pltpu.VMEM((2 * NT, LANES), F32),
            pltpu.VMEM((2 * NT, LANES), F32),
            pltpu.VMEM((2, NT, LANES), BF16),
            pltpu.VMEM((2, NT, LANES), BF16),
            pltpu.VMEM((2 * NT // 256, 8, LANES), BF16),
            pltpu.VMEM((2, 2 * NT // 256, 8, LANES), BF16),
            pltpu.VMEM((2, NT, LANES), F32),
            pltpu.VMEM((2, NFFT * PITCH, LANES), F32),
            pltpu.VMEM((2, 2 * BATCH * NB, 2 * LANES), BF16),
            pltpu.VMEM((2, NBATCH, 2 * BATCH * NB, 2 * LANES), BF16),
            pltpu.VMEM((2, 2 * BATCH * NB, 2 * LANES), BF16),
            pltpu.VMEM((2 * NBATCH, NB, LANES), F32),
            pltpu.VMEM((GROUP, 8, LANES), F32),
            pltpu.VMEM((GROUP, 8, LANES), F32),
            pltpu.VMEM((NZ, 8, LANES), F32),
            pltpu.VMEM((GROUP, 2, LANES), F32),
            pltpu.VMEM((2, LANES), F32),
            dma((8,)),
            dma((2, 4)), dma((2, 4)), dma((2,)), dma((2,)),
            dma(()), dma(()), dma(()), dma(()), dma(()), dma(()),
        ],
        compiler_params=pltpu.CompilerParams(
            collective_id=0, has_side_effects=True, vmem_limit_bytes=48 * 1024 * 1024
        ),
        name="bispectrum",
    )(
        *[
            pltpu.with_memory_space_constraint(array, pltpu.HBM)
            for array in (u_rows, v_rows, transform, hann, cell_weights, block_offsets, triads.T)
        ]
    )
    return values.T, fields.reshape(NTRI, 2, 2, LANES)


def solution(mesh):
    return jax.shard_map(
        on_device,
        mesh=mesh,
        in_specs=(P(None, "space", "freq"), P(None, "space", "freq"), P("space", "freq"), P(), P()),
        out_specs=(P(), P(None, None, "space", "freq")),
        check_vma=False,
    )
```

```python
import math

import jax
import jax.numpy as jnp
import numpy as np
from jax import lax
from jax.experimental import pallas as pl
from jax.experimental.pallas import tpu as pltpu
from jax.sharding import PartitionSpec as P

NFFT = 256
HALF = NFFT // 2
NB = 16
PITCH = 17
POW = 4
NT = 2176
LANES = 128
NTRI = 64
NZ = 8
GROUP = 32
PER_Z = 8
NFREQ = 4
BATCH = 8
NBATCH = NTRI // BATCH
SUB = 64
CHUNKS = ((0, 256), (256, 640), (896, 832), (1728, 448))
F32 = jnp.float32
BF16 = jnp.bfloat16


def tables():
    times = np.arange(NFFT)
    freqs = np.arange(HALF)
    angles = (freqs[:, None] * times[None, :] % NFFT).astype(np.float32) * np.float32(2.0 * math.pi / NFFT)
    window = (0.5 - 0.5 * np.cos(times * (2.0 * math.pi / NFFT))).astype(np.float32)
    scaling = np.float32(1.0 / np.sqrt(np.sum(window.astype(np.float64) ** 2)))
    transform = np.concatenate(
        [np.cos(angles.astype(np.float64)) * scaling, -np.sin(angles.astype(np.float64)) * scaling], axis=0
    )
    hann = np.ascontiguousarray(np.broadcast_to(window[:, None], (NFFT, LANES)))
    return transform.astype(jnp.bfloat16), hann


def dot_nt(lhs, rhs):
    return lax.dot_general(lhs, rhs, (((1,), (1,)), ((), ())), preferred_element_type=F32)


def dot_nn(lhs, rhs):
    return lax.dot_general(lhs, rhs, (((1,), (0,)), ((), ())), preferred_element_type=F32)


def split(value):
    high = value.astype(BF16)
    return high, (value - high.astype(F32)).astype(BF16)


def swap16(value, lane):
    return jnp.where(
        (lane // 16) % 2 == 0, pltpu.roll(value, LANES - 16, value.ndim - 1), pltpu.roll(value, 16, value.ndim - 1)
    )


def kernel(
    u_hbm, v_hbm, table_hbm, hann_hbm, w_ref, offs, tri,
    modes_ref, vals_ref,
    ubuf, vbuf, table, hann, vf, duf, snd, halo, colsend, colrecv, vort, spec,
    lhs, rhi, rlo, cross, pieces, recv1, recv2, recv3, out3,
    load_sem, vsend, vrecv, usend, urecv, s1, r1, s2, r2, s3, r3,
):
    sp = lax.axis_index("space")
    fq = lax.axis_index("freq")
    core = sp % 2
    zi = sp // PER_Z
    xi = (sp // 2) % 4
    inz = sp % PER_Z
    me = inz * NFREQ + fq
    sibling = sp + 1 - 2 * core
    outer = (sp + 63 + 2 * core) % 64
    cores = [core, 1 - core]
    xs = [xi] + [(xi + d) % 4 for d in (1, 2, 3)]
    ys = [fq] + [(fq + d) % NFREQ for d in (1, 2, 3)]
    zs = [zi] + [(zi + d) % NZ for d in range(1, NZ)]
    x_slow = core
    x_fast = 1 - core
    sign = (1 - 2 * core).astype(F32)

    def device(space, freq):
        return {"device_id": {"space": space, "freq": freq}, "device_id_type": pl.DeviceIdType.MESH}

    loads_v = []
    for n, (t0, cnt) in enumerate(CHUNKS):
        rows = pl.ds(2 * t0, 2 * cnt)
        loads_v.append(pltpu.make_async_copy(v_hbm.at[rows], vbuf.at[rows], load_sem.at[n]))
    load_u = pltpu.make_async_copy(u_hbm, ubuf, load_sem.at[4])
    load_h = pltpu.make_async_copy(hann_hbm, hann, load_sem.at[6])
    load_t = pltpu.make_async_copy(table_hbm, table, load_sem.at[7])
    loads_v[0].start()
    for load in loads_v[1:]:
        load.start()
    load_u.start()
    load_h.start()
    load_t.start()

    barrier = pltpu.get_barrier_semaphore()
    pl.semaphore_signal(barrier, inc=1, **device(outer, fq))
    for dz in (4, 3, 5, 2, 6, 1, 7):
        pl.semaphore_signal(barrier, inc=1, **device(zs[dz] * PER_Z + inz, fq))
    plane_spaces = {(dx, dc): zi * PER_Z + xs[dx] * 2 + cores[dc] for dx in range(4) for dc in (0, 1)}
    far_first = sorted(
        ((dx, dc, dy) for dx in range(4) for dc in (0, 1) for dy in range(4) if dx or dc or dy),
        key=lambda step: -(min(step[0], 4 - step[0]) + min(step[2], 4 - step[2])),
    )
    for dx, dc, dy in far_first:
        pl.semaphore_signal(barrier, inc=1, **device(plane_spaces[dx, dc], ys[dy]))

    def unpack(n):
        t0, cnt = CHUNKS[n]
        loads_v[n].wait()

        @pl.loop(t0 // SUB, (t0 + cnt) // SUB)
        def _(i):
            both = pl.ds(pl.multiple_of(i * 2 * SUB, 2 * SUB), 2 * SUB)
            one = pl.ds(pl.multiple_of(i * SUB, SUB), SUB)
            vf[both, :] = vbuf[both, :].astype(F32)
            snd[1, one, :] = vf[pl.ds(i * 2 * SUB + x_slow, SUB, stride=2), :].astype(BF16)
            snd[0, one, :] = vf[pl.ds(i * 2 * SUB + x_fast, SUB, stride=2), :].astype(BF16)

    copies_v = {}

    def send(n, plane, target):
        rows = pl.ds(CHUNKS[n][0], CHUNKS[n][1])
        copies_v[n, plane] = pltpu.make_async_remote_copy(
            src_ref=snd.at[plane, rows], dst_ref=halo.at[plane, rows],
            send_sem=vsend.at[plane, n], recv_sem=vrecv.at[plane, n], **device(target, fq),
        )
        copies_v[n, plane].start()

    lane8 = lax.broadcasted_iota(jnp.int32, (8, LANES), 1)
    pair8 = lane8 // 2
    rowm = lax.broadcasted_iota(jnp.int32, (LANES, LANES), 0)
    lanem = lax.broadcasted_iota(jnp.int32, (LANES, LANES), 1)
    pick = jnp.where(rowm == jnp.where(lanem % 2 == 0, LANES - 1, 0), 1.0, 0.0).astype(BF16)
    diff = jnp.where(rowm == lanem + 1, 0.5, jnp.where(rowm == lanem - 1, -0.5, 0.0)).astype(BF16)
    place = jnp.where(rowm % 2 == 0, jnp.where(lanem == 0, -0.5, 0.0), jnp.where(lanem == LANES - 1, 0.5, 0.0))
    diff = jnp.concatenate([diff, place.astype(BF16)], axis=0)

    unpack(0)
    pl.semaphore_wait(barrier, GROUP - 1 + NZ - 1 + 1)
    send(0, 1, outer)
    send(0, 0, sibling)
    load_u.wait()

    @pl.loop(0, 2 * NT // 256, unroll=True)
    def _(g):
        spread = dot_nn(ubuf[pl.ds(pl.multiple_of(g * 256, 256), 256), :], pick)
        packed = jnp.zeros((8, LANES), F32)
        for i in range(32):
            packed = jnp.where(pair8 == i, spread[8 * i:8 * i + 8], packed)
        colsend[g] = packed.astype(BF16)

    copies_u = []
    for slot, target in ((1, ys[3]), (0, ys[1])):
        copies_u.append(
            pltpu.make_async_remote_copy(
                src_ref=colsend, dst_ref=colrecv.at[slot],
                send_sem=usend.at[slot], recv_sem=urecv.at[slot], **device(sp, target),
            )
        )
        copies_u[-1].start()
    for n in range(1, len(CHUNKS)):
        unpack(n)
        send(n, 1, outer)
    for n in range(1, len(CHUNKS)):
        send(n, 0, sibling)

    has_left = (fq > 0).astype(F32)
    has_right = (fq < NFREQ - 1).astype(F32)
    for copy in copies_u:
        copy.wait()

    @pl.loop(0, 2 * NT // 256, unroll=True)
    def _(g):
        from_left = colrecv[0, g].astype(F32) * has_left
        from_right = colrecv[1, g].astype(F32) * has_right
        packed = jnp.where(lane8 % 2 == 0, from_left, from_right)
        edges = jnp.concatenate([jnp.where(pair8 == i, packed, 0.0) for i in range(32)], axis=0).astype(BF16)
        rows = pl.ds(pl.multiple_of(g * 256, 256), 256)
        duf[rows, :] = dot_nn(jnp.concatenate([ubuf[rows, :], edges], axis=1), diff)

    load_h.wait()
    load_t.wait()
    lane = lax.broadcasted_iota(jnp.int32, (16, LANES), 1)
    quarter = lane // 32
    has_outer = jnp.where(core == 0, sp > 0, sp < 63).astype(F32)

    for plane in (0, 1):
        own = x_fast if plane == 0 else x_slow
        half = 0.5 * sign if plane == 0 else -0.5 * sign
        mask = 1.0 if plane == 0 else has_outer
        total = jnp.zeros((8, LANES), F32)
        for n, (t0, cnt) in enumerate(CHUNKS):
            copies_v[n, plane].wait()

            def vorticity(i, total):
                one = pl.ds(pl.multiple_of(i * SUB, SUB), SUB)
                far = halo[plane, one, :].astype(F32) * mask
                near = snd[1 - plane, one, :].astype(F32)
                value = half * (far - near) - duf[pl.ds(i * 2 * SUB + own, SUB, stride=2), :]
                vort[plane, one, :] = value
                return total + jnp.sum(value.reshape(SUB // 8, 8, LANES), axis=0)

            total = lax.fori_loop(t0 // SUB, (t0 + cnt) // SUB, vorticity, total, unroll=True)
        mean = jnp.sum(total, axis=0, keepdims=True) * (1.0 / NT)

        @pl.loop(0, NB // 4, unroll=True)
        def _(four):
            for h in (0, 1):
                parts = []
                for k in (0, 1):
                    block = vort[plane, pl.ds(offs[4 * four + 2 * h + k], NFFT), :]
                    parts.append(((block - mean) * hann[...]).astype(BF16))
                out = dot_nn(table[...], jnp.concatenate(parts, axis=1))
                for k in (0, 1):
                    spec[plane, pl.ds(4 * four + 2 * h + k, NFFT, stride=PITCH), :] = out[:, k * LANES:(k + 1) * LANES]

        weight = w_ref[pl.ds(own, 1), :]

        waiting = []
        for step in range(4):
            x_to = xs[3 - step]
            for dc in (1, 0):
                batch = x_to * 2 + cores[dc]
                for i in range(BATCH):
                    j = batch * BATCH + i
                    k_at = tri[0, j]
                    l_at = tri[1, j]

                    def rows_of(f):
                        return spec[plane, pl.ds(f * PITCH, NB), :]

                    k_re, k_im = rows_of(k_at), rows_of(k_at + HALF)
                    l_re, l_im = rows_of(l_at), rows_of(l_at + HALF)
                    t_re, t_im = rows_of(k_at + l_at), rows_of(k_at + l_at + HALF)
                    p_re = (k_re * l_re - k_im * l_im) * weight
                    p_im = (k_re * l_im + k_im * l_re) * weight
                    for c, value in ((0, p_re), (1, p_im)):
                        high, low = split(value)
                        lhs[dc, i * NB:(i + 1) * NB, c * LANES:(c + 1) * LANES] = high
                        lhs[dc, 128 + i * NB:128 + (i + 1) * NB, c * LANES:(c + 1) * LANES] = low
                    re_hi, re_lo = split(t_re)
                    im_hi, im_lo = split(t_im)
                    at_re = slice(2 * i * NB, (2 * i + 1) * NB)
                    at_im = slice((2 * i + 1) * NB, (2 * i + 2) * NB)
                    rhi[plane, batch, at_re, 0:LANES] = re_hi
                    rhi[plane, batch, at_im, 0:LANES] = im_hi
                    rhi[plane, batch, at_re, LANES:] = im_hi
                    rhi[plane, batch, at_im, LANES:] = -re_hi
                    rlo[dc, at_re, 0:LANES] = re_lo
                    rlo[dc, at_im, 0:LANES] = im_lo
                    rlo[dc, at_re, LANES:] = im_lo
                    rlo[dc, at_im, LANES:] = -re_lo
                out = dot_nt(lhs[dc], rhi[plane, batch])
                out = out[0:128] + out[128:256] + dot_nt(lhs[dc, 0:128], rlo[dc])
                for h in (0, 1):
                    cols = slice(h * LANES, (h + 1) * LANES)
                    acc = out[h * 64:h * 64 + 16, cols]
                    for i in (1, 2, 3):
                        acc = jnp.where(quarter == i, out[h * 64 + i * 16:h * 64 + i * 16 + 16, cols], acc)
                    if plane == 0:
                        cross[2 * batch + h] = acc
                    else:
                        acc = acc + cross[2 * batch + h]
                        low, high = acc[0:8], acc[8:16]
                        first = lane[0:8] < 64
                        pieces[4 * batch + 2 * h] = jnp.where(first, low, pltpu.roll(high, 64, 1))
                        pieces[4 * batch + 2 * h + 1] = jnp.where(first, pltpu.roll(low, 64, 1), high)
                if plane == 1:
                    waiting.append([
                        pltpu.make_async_remote_copy(
                            src_ref=pieces.at[4 * batch + ys[dy]], dst_ref=recv1.at[(3 - step) * 8 + dc * 4 + dy],
                            send_sem=s1, recv_sem=r1, **device(zi * PER_Z + batch, ys[dy]),
                        )
                        for dy in (2, 1, 3, 0)
                        if step < 3 or dc or dy
                    ])
                    if len(waiting) > 0:
                        for copy in waiting.pop(0):
                            copy.start()
        for copies in waiting:
            for copy in copies:
                copy.start()

    pltpu.make_async_copy(recv1.at[pl.ds(1, GROUP - 1)], recv1.at[pl.ds(1, GROUP - 1)], r1).wait()
    own_sum = pieces[me]
    for d in range(1, GROUP):
        own_sum = own_sum + recv1[d]
    recv2[zi] = own_sum

    for dz in (4, 3, 5, 2, 6, 1, 7):
        pltpu.make_async_remote_copy(
            src_ref=recv2.at[zi], dst_ref=recv2.at[zi], send_sem=s2, recv_sem=r2,
            **device(zs[dz] * PER_Z + inz, fq),
        ).start()
    pltpu.make_async_copy(recv2.at[pl.ds(0, NZ - 1)], recv2.at[pl.ds(0, NZ - 1)], r2).wait()
    both = recv2[0]
    for z in range(1, NZ):
        both = both + recv2[z]
    both = both * (1.0 / (NB * math.sqrt(128 * 512)))

    c16 = jnp.concatenate([both, pltpu.roll(both, 64, 1)], axis=0)
    c16 = jnp.where(lane < 64, c16, 0.0)
    odd = (lane // 16) % 2 == 1
    mat = jnp.concatenate([jnp.where(odd, -c16, c16), swap16(c16, lane)], axis=0)
    turned = jnp.concatenate([mat, jnp.zeros((96, LANES), F32)], axis=0).T
    lane32 = lax.broadcasted_iota(jnp.int32, (32, LANES), 1)
    row32 = lax.broadcasted_iota(jnp.int32, (32, LANES), 0)
    lane1 = lax.broadcasted_iota(jnp.int32, (1, LANES), 1)
    mat_t = jnp.where(lane32 < 32, turned[0:32], pltpu.roll(turned[32:64], 32, 1))

    def by_triad(value, lanes):
        first = jnp.sum(jnp.where(lanes < 32, value, 0.0), axis=1, keepdims=True)
        second = jnp.sum(jnp.where((lanes >= 32) & (lanes < 64), value, 0.0), axis=1, keepdims=True)
        return jnp.where(lanes < 32, first, second)

    def to_lanes(vec):
        return jnp.sum(mat_t * vec, axis=0, keepdims=True)

    vec = jnp.where(row32 < 16, 1.0 / math.sqrt(NB), 0.0).astype(F32)
    for _ in range(POW // 2):
        out = to_lanes(vec)
        out = out / jnp.sqrt(by_triad(out * out, lane1))
        vec = by_triad(mat * out, lane32)
        vec = vec / jnp.sqrt(jnp.sum(vec * vec, axis=0, keepdims=True))
    out = to_lanes(vec)
    lead = jnp.where(lane1 < 64, jnp.sum(jnp.where(lane32 % 32 == row32, vec, 0.0), axis=0, keepdims=True), 0.0)
    val_re = by_triad(lead * out, lane1)
    crossed = lead * swap16(out, lane1)
    val_im = by_triad(jnp.where((lane1 // 16) % 2 == 0, crossed, -crossed), lane1)
    spot = lane1 - 2 * me
    re0, re1 = val_re[:, 0:1], val_re[:, 32:33]
    im0, im1 = val_im[:, 0:1], val_im[:, 32:33]
    vals = jnp.where(spot == 0, re0, jnp.where(spot == 1, re1, 0.0))
    vals = vals + jnp.where(spot == 64, im0, jnp.where(spot == 65, im1, 0.0))
    placed = jnp.where((me % 2) == 1, pltpu.roll(lead, 64, 1), lead)
    out3[...] = jnp.concatenate([placed, vals], axis=0)
    recv3[me] = out3[...]

    for dx, dc, dy in far_first:
        pltpu.make_async_remote_copy(
            src_ref=out3, dst_ref=recv3.at[me], send_sem=s3, recv_sem=r3, **device(plane_spaces[dx, dc], ys[dy])
        ).start()
    row_lhs = lax.broadcasted_iota(jnp.int32, (16, 2 * LANES), 0)
    lane_lhs = lax.broadcasted_iota(jnp.int32, (16, 2 * LANES), 1)
    live = lane_lhs // 32 == row_lhs // 2
    pltpu.make_async_copy(recv3.at[pl.ds(0, GROUP - 1)], recv3.at[pl.ds(0, GROUP - 1)], r3).wait()

    vals_all = recv3[0][1:2]
    for q in range(1, GROUP):
        vals_all = vals_all + recv3[q][1:2]
    vals_ref[...] = jnp.concatenate([vals_all, pltpu.roll(vals_all, 64, 1)], axis=0)[:, 0:NTRI]

    @pl.loop(0, NBATCH // 2, unroll=True)
    def _(pair):
        for k in (0, 1):
            batch = 2 * pair + k
            parts = [recv3[4 * batch + 2 * h][0:1] + recv3[4 * batch + 2 * h + 1][0:1] for h in (0, 1)]
            flat = jnp.concatenate([jnp.where((lane1 // 16) % 2 == 1, -p, p) for p in parts], axis=1)
            turned = jnp.concatenate([swap16(p, lane1) for p in parts], axis=1)
            coeff = jnp.where(live, jnp.where(row_lhs % 2 == 0, flat, turned), 0.0)
            high, low = split(coeff)
            stacked = jnp.concatenate([high, low], axis=0)
            fields = jnp.concatenate([rhi[0, batch, :, 0:LANES], rhi[1, batch, :, 0:LANES]], axis=1)
            res = dot_nn(stacked, fields)
            res = res[0:16] + res[16:32]
            modes_ref[pl.ds(batch * 32 + x_fast, 16, stride=2), :] = res[:, 0:LANES]
            modes_ref[pl.ds(batch * 32 + x_slow, 16, stride=2), :] = res[:, LANES:]

    pltpu.make_async_copy(recv1.at[pl.ds(1, GROUP - 1)], recv1.at[pl.ds(1, GROUP - 1)], s1).wait()
    pltpu.make_async_copy(recv2.at[pl.ds(0, NZ - 1)], recv2.at[pl.ds(0, NZ - 1)], s2).wait()
    pltpu.make_async_copy(recv3.at[pl.ds(0, GROUP - 1)], recv3.at[pl.ds(0, GROUP - 1)], s3).wait()


def on_device(u_velocity, v_velocity, cell_weights, block_offsets, triads):
    transform, hann = tables()
    u_rows = u_velocity.reshape(2 * NT, LANES)
    v_rows = v_velocity.reshape(2 * NT, LANES)
    anywhere = pl.BlockSpec(memory_space=pltpu.HBM)
    vmem = pl.BlockSpec(memory_space=pltpu.VMEM)
    smem = pl.BlockSpec(memory_space=pltpu.SMEM)
    dma = pltpu.SemaphoreType.DMA
    fields, values = pl.pallas_call(
        kernel,
        out_shape=(jax.ShapeDtypeStruct((4 * NTRI, LANES), F32), jax.ShapeDtypeStruct((2, NTRI), F32)),
        in_specs=[anywhere] * 4 + [vmem, smem, smem],
        out_specs=(vmem, vmem),
        scratch_shapes=[
            pltpu.VMEM((2 * NT, LANES), BF16),
            pltpu.VMEM((2 * NT, LANES), BF16),
            pltpu.VMEM((NFFT, NFFT), BF16),
            pltpu.VMEM((NFFT, LANES), F32),
            pltpu.VMEM((2 * NT, LANES), F32),
            pltpu.VMEM((2 * NT, LANES), F32),
            pltpu.VMEM((2, NT, LANES), BF16),
            pltpu.VMEM((2, NT, LANES), BF16),
            pltpu.VMEM((2 * NT // 256, 8, LANES), BF16),
            pltpu.VMEM((2, 2 * NT // 256, 8, LANES), BF16),
            pltpu.VMEM((2, NT, LANES), F32),
            pltpu.VMEM((2, NFFT * PITCH, LANES), F32),
            pltpu.VMEM((2, 2 * BATCH * NB, 2 * LANES), BF16),
            pltpu.VMEM((2, NBATCH, 2 * BATCH * NB, 2 * LANES), BF16),
            pltpu.VMEM((2, 2 * BATCH * NB, 2 * LANES), BF16),
            pltpu.VMEM((2 * NBATCH, NB, LANES), F32),
            pltpu.VMEM((GROUP, 8, LANES), F32),
            pltpu.VMEM((GROUP, 8, LANES), F32),
            pltpu.VMEM((NZ, 8, LANES), F32),
            pltpu.VMEM((GROUP, 2, LANES), F32),
            pltpu.VMEM((2, LANES), F32),
            dma((8,)),
            dma((2, 4)), dma((2, 4)), dma((2,)), dma((2,)),
            dma(()), dma(()), dma(()), dma(()), dma(()), dma(()),
        ],
        compiler_params=pltpu.CompilerParams(
            collective_id=0, has_side_effects=True, vmem_limit_bytes=48 * 1024 * 1024
        ),
        name="bispectrum",
    )(
        *[
            pltpu.with_memory_space_constraint(array, pltpu.HBM)
            for array in (u_rows, v_rows, transform, hann, cell_weights, block_offsets, triads.T)
        ]
    )
    return values.T, fields.reshape(NTRI, 2, 2, LANES)


def solution(mesh):
    return jax.shard_map(
        on_device,
        mesh=mesh,
        in_specs=(P(None, "space", "freq"), P(None, "space", "freq"), P("space", "freq"), P(), P()),
        out_specs=(P(), P(None, None, "space", "freq")),
        check_vma=False,
    )
```
